128 devices in a mesh: scene: 16 (over y, z_hi, core), batch: 8 (over x, z_lo).
Axes of the slice: x: 4, y: 4, z: 4 (z_hi: 2, z_lo: 2; z = z_hi * 2 + z_lo), core: 2. Of those that a mesh axis runs over, the one named last changes fastest.
Arguments:
- tokens: float32 [8, 6144, 384], P('batch', 'scene'), may hold values from -6 to 6
- nbr_offset: int32 [27, 8, 6144], P(None, 'batch', 'scene'), may hold values from -64 to 65, as said below
- cotangent: float32 [8, 6144, 384], P('batch', 'scene'), may hold values from -6 to 6
- conv_weight: float32 [27, 384], replicated, may hold values from -1.25 to 1.25
- w_qkv: float32 [384, 1152], replicated, may hold values from -0.3125 to 0.3125
- w_out: float32 [384, 384], replicated, may hold values from -0.3125 to 0.3125
- score_bias: float32 [24, 32, 32], replicated, may hold values from -6 to 400
- w_up: float32 [384, 1536], replicated, may hold values from -0.3125 to 0.3125
- w_down: float32 [1536, 384], replicated, may hold values from -0.15625 to 0.15625
Outputs:
- block_out: float32 [8, 6144, 384], P('batch', 'scene')
- grad_mid: float32 [8, 6144, 384], P('batch', 'scene')
- grad_up: float32 [384, 1536], P('scene', 'batch')
- grad_down: float32 [1536, 384], P('scene', 'batch')
The draws below stay inside these ranges and needn't reach their ends.
Inputs may be any that keep to these rules, and one draw needn't show every extreme that they name: `nbr_offset`: the middle tap is 0 for every token; the value 64 + 1 marks a missing neighbour.
All inputs are finite; a program needn't handle non-finite values.
Results may differ from the reference program's by a relative error of at most 0.000075.
Values sent between devices are 32-bit elements; how exact they have to be, the bound alone decides.
No kernel may reach another device: no remote copies, remote signals or barrier semaphores. Data moves between devices by JAX's collectives and lax.ppermute only.
A program may use at most 128 MiB of HBM per device.

```python
import jax
import jax.numpy as jnp
from jax import lax

D = 384
FF = 1536
HEADS = 24
GROUP = 32
TAPS = 27
HALO = 64
SEQ = 6144
BATCHES = 8
STRIDE = 192


def draw_nbr_offset(key, part):
    offsets = jax.random.randint(key, (TAPS, BATCHES, SEQ), -HALO, HALO + 2, dtype=jnp.int32)
    offsets = offsets.at[TAPS // 2].set(0)
    offsets = offsets.at[0, 0, 0].set(-HALO)
    offsets = offsets.at[1, 0, 0].set(HALO + 1)
    return offsets


def draw_score_bias(key, part):
    base_key = jax.random.fold_in(key, 0)
    values = jnp.clip(jax.random.normal(base_key, (HEADS, GROUP, GROUP), jnp.float32), -6.0, 6.0)
    return values


def level_of(rng, extent, shards, low, largest):
    level, own = 1.0, jax.random.fold_in(rng, 6)
    for position, shards_of in shards:
        heights = jnp.exp(jax.random.uniform(jax.random.fold_in(own, position), (shards_of,), jnp.float32, low / len(shards), largest / len(shards)))
        level = level * jnp.repeat(heights, extent[position] // shards_of).reshape([-1 if axis == position else 1 for axis in range(len(extent))])
    return level


def centred(own_key, extent, width, limit, cuts=(), held_as=jnp.bfloat16):
    entries = width * jax.random.normal(own_key, extent, jnp.float32)
    if cuts:
        entries = entries * level_of(own_key, extent, cuts, -0.22, 0.18)
    return jnp.clip(entries, -limit, limit).astype(held_as)


def setup_inputs(seed: int = 0) -> dict:
    key_of = jax.random.split(jax.random.key(seed), 10)
    tokens = centred(key_of[0], (BATCHES, SEQ, D), 1.0, 6.0, ((0, 8), (1, 16)), jnp.float32)
    nbr_offset = draw_nbr_offset(jax.random.fold_in(key_of[9], 71), 0)
    cotangent = centred(key_of[2], (BATCHES, SEQ, D), 1.0, 6.0, ((0, 8), (1, 16)), jnp.float32)
    conv_weight = centred(key_of[3], (TAPS, D), TAPS ** -0.5, 1.25, (), jnp.float32)
    w_qkv = centred(key_of[4], (D, 3 * D), D ** -0.5, 0.3125, (), jnp.float32)
    w_out = centred(key_of[5], (D, D), D ** -0.5, 0.3125, (), jnp.float32)
    score_bias = draw_score_bias(jax.random.fold_in(key_of[9], 71), 0)
    w_up = centred(key_of[7], (D, FF), D ** -0.5, 0.3125, (), jnp.float32)
    w_down = centred(key_of[8], (FF, D), FF ** -0.5, 0.15625, (), jnp.float32)
    return {"tokens": tokens, "nbr_offset": nbr_offset, "cotangent": cotangent, "conv_weight": conv_weight, "w_qkv": w_qkv, "w_out": w_out, "score_bias": score_bias, "w_up": w_up, "w_down": w_down}


def layer_norm(values):
    average = lax.optimization_barrier(jnp.mean(values, axis=-1, keepdims=True))
    centered = values - average
    variance = lax.optimization_barrier(jnp.mean(centered * centered, axis=-1, keepdims=True))
    return centered * lax.rsqrt(variance + 1e-05)

def group_attention(members, score_bias):
    count, slots, channels = members.shape
    feature_width = channels // 3
    head_count = score_bias.shape[0]
    head_dim = feature_width // head_count
    query = members[:, :, :feature_width].reshape(count, slots, head_count, head_dim)
    keys = members[:, :, feature_width:2 * feature_width].reshape(count, slots, head_count, head_dim)
    values = members[:, :, 2 * feature_width:].reshape(count, slots, head_count, head_dim)
    scores = jnp.einsum('nihd,njhd->nhij', query, keys, precision=lax.Precision.HIGHEST) * head_dim ** (-0.5)
    scores = scores + score_bias[None]
    weights = jax.nn.softmax(scores, axis=-1)
    mixed = jnp.einsum('nhij,njhd->nihd', weights, values, precision=lax.Precision.HIGHEST)
    return mixed.reshape(count, slots, feature_width)

def mlp_branch(middle, w_up, w_down):
    normed = layer_norm(middle)
    hidden = jnp.dot(normed, w_up, precision=lax.Precision.HIGHEST, preferred_element_type=jnp.float32)
    activation = jax.nn.gelu(hidden, approximate=False)
    return middle + jnp.dot(activation, w_down, precision=lax.Precision.HIGHEST, preferred_element_type=jnp.float32)

def reference(tokens, nbr_offset, cotangent, conv_weight, w_qkv, w_out, score_bias, w_up, w_down):
    feature_width = tokens.shape[2]
    positions = jnp.arange(SEQ, dtype=jnp.int32)
    padded = jnp.pad(tokens, ((0, 0), (HALO, HALO + 1), (0, 0)))
    stencil = jnp.zeros_like(tokens)
    for tap_index in range(TAPS):
        offsets = nbr_offset[tap_index]
        row_index = jnp.where(offsets > HALO, SEQ + 2 * HALO, positions[None, :] + HALO + offsets).astype(jnp.int32)
        picked = jax.vmap(lambda table, where_rows: table[where_rows])(padded, row_index)
        stencil = stencil + picked * conv_weight[tap_index]
    first = tokens + stencil
    normed = layer_norm(first).reshape(BATCHES * SEQ, feature_width)
    qkv = jnp.dot(normed, w_qkv, precision=lax.Precision.HIGHEST, preferred_element_type=jnp.float32)
    grouped = qkv.reshape(BATCHES, GROUP, STRIDE, 3 * feature_width).transpose(0, 2, 1, 3)
    grouped = grouped.reshape(BATCHES * STRIDE, GROUP, 3 * feature_width)
    attended = group_attention(grouped, score_bias)
    attended = attended.reshape(BATCHES, STRIDE, GROUP, feature_width).transpose(0, 2, 1, 3)
    attended = attended.reshape(BATCHES * SEQ, feature_width)
    middle = first.reshape(BATCHES * SEQ, feature_width) + jnp.dot(attended, w_out, precision=lax.Precision.HIGHEST, preferred_element_type=jnp.float32)
    block_out, pullback = jax.vjp(mlp_branch, middle, w_up, w_down)
    grad_mid, grad_up, grad_down = pullback(cotangent.reshape(BATCHES * SEQ, feature_width))
    grad_scale = lax.rsqrt(jnp.asarray(BATCHES * SEQ, jnp.float32))
    return (block_out.reshape(BATCHES, SEQ, feature_width), grad_mid.reshape(BATCHES, SEQ, feature_width), grad_up * grad_scale, grad_down * grad_scale)
```

```python
import functools

import jax
import jax.numpy as jnp
from jax import lax
from jax.experimental import pallas as pl
from jax.experimental.pallas import tpu as pltpu
from jax.sharding import Mesh
from jax.sharding import PartitionSpec as P

D = 384
FF = 1536
TAPS = 27
HALO = 64
TOK = 384
SCENE = 16
UNITS = 24
HALF = FF // 2
SCENE_AXES = ("y", "zh", "c")
BATCH_AXES = ("x", "zl")
CHIP_AXES = ("y", "zh", "x", "zl")
F32 = jnp.float32
BF16 = jnp.bfloat16
NN = (((1,), (0,)), ((), ()))
NT = (((1,), (1,)), ((), ()))
VMEM_SPEC = pl.BlockSpec(memory_space=pltpu.VMEM)
PARAMS = pltpu.CompilerParams(vmem_limit_bytes=58 * 1024 * 1024)


def parts_of(values):
    high = values.astype(BF16)
    return high, (values - high.astype(F32)).astype(BF16)


def dot(a, b, dims=NN):
    return lax.dot_general(a, b, dims, preferred_element_type=F32)


def dot3(a, b, dims=NN):
    return dot(a[0], b[0], dims) + (dot(a[0], b[1], dims) + dot(a[1], b[0], dims))


def normalise(values):
    average = jnp.mean(values, axis=-1, keepdims=True)
    centered = values - average
    variance = jnp.mean(centered * centered, axis=-1, keepdims=True)
    scale = lax.rsqrt(variance + 1e-05)
    return centered * scale, scale


def by_unit(ref):
    rows = []
    for unit in range(UNITS):
        tiles = [ref[pl.ds(UNITS * t + unit, SCENE, stride=3 * UNITS), :] for t in range(3)]
        rows.append(jnp.concatenate(tiles, axis=1))
    return jnp.concatenate(rows, axis=0)


def by_member(ref, values):
    for unit in range(UNITS):
        for t in range(3):
            ref[pl.ds(UNITS * t + unit, SCENE, stride=3 * UNITS), :] = values[
                SCENE * unit : SCENE * (unit + 1), 128 * t : 128 * (t + 1)
            ]


def conv_kernel(tok_ref, low_ref, high_ref, nbr_ref, weight_ref, sent_ref):
    middle_tap = TAPS // 2
    taps = [a for a in range(TAPS) if a != middle_tap]
    chunk = 13
    tok = tok_ref[...]
    ext = jnp.concatenate([low_ref[...], tok, high_ref[...]], axis=0)
    ext_high, ext_low = parts_of(ext)
    offsets = jnp.concatenate([nbr_ref[:, 0, :], jnp.zeros((5, TOK), jnp.int32)], axis=0).T
    row = lax.broadcasted_iota(jnp.int32, (128, 32), 0)
    lanes = lax.broadcasted_iota(jnp.int32, (128, 256), 1)
    done = []
    for block in range(3):
        rows = slice(128 * block, 128 * (block + 1))
        window = slice(128 * block, 128 * block + 256)
        table = jnp.concatenate([ext_high[window], ext_low[window]], axis=1)
        off = offsets[rows]
        index = jnp.where(off > HALO, -1, off + row + HALO)
        acc = tok[rows] + tok[rows] * weight_ref[middle_tap : middle_tap + 1, :]
        for start in range(0, len(taps), chunk):
            hits = [
                jnp.where(index[:, a : a + 1] == lanes, 1.0, 0.0).astype(BF16)
                for a in taps[start : start + chunk]
            ]
            picked = dot(jnp.concatenate(hits, axis=0), table)
            for i, a in enumerate(taps[start : start + chunk]):
                piece = picked[128 * i : 128 * (i + 1)]
                acc = acc + (piece[:, :D] + piece[:, D:]) * weight_ref[a : a + 1, :]
        done.append(acc)
    by_member(sent_ref, jnp.concatenate(done, axis=0))


def attention_kernel(got_ref, qkv_ref, wout_ref, bias_ref, sent_ref, scores_ref):
    normed, _ = normalise(by_unit(got_ref))
    qkv = dot3(parts_of(normed), parts_of(qkv_ref[...]))
    bias = bias_ref[...]
    lane = lax.broadcasted_iota(jnp.int32, (16, 128), 1)
    head_of = lane // 16
    row_head = (lax.broadcasted_iota(jnp.int32, (256, 128), 0) // 16) % 8
    ones = jnp.where(row_head == lax.broadcasted_iota(jnp.int32, (256, 128), 1) // 16, 1.0, 0.0).astype(BF16)
    lane_all = lax.broadcasted_iota(jnp.int32, (TOK, 128), 1)

    def members(values, group):
        return values[16 * group : 16 * group + 16], values[192 + 16 * group : 208 + 16 * group]

    def spread(values, group):
        pieces = []
        for piece in members(values, group):
            pieces += [jnp.where(head_of == h, piece, 0.0) for h in range(8)]
        return parts_of(jnp.concatenate(pieces, axis=0))

    attended = []
    for t in range(3):
        cols = slice(128 * t, 128 * (t + 1))
        query = qkv[:, :D][:, cols] * 0.25
        keys = qkv[:, D : 2 * D][:, cols]
        vals = qkv[:, 2 * D :][:, cols]
        for g in range(12):
            q_high, q_low = parts_of(jnp.concatenate(members(query, g), axis=0))
            k_high, k_low = spread(keys, g)
            both = dot(jnp.concatenate([q_high, q_low], axis=0), k_high, NT)
            score = both[:32] + (both[32:] + dot(q_high, k_low, NT))
            scores_ref[32 * g : 32 * g + 32, :] = score + bias[:, 256 * t : 256 * (t + 1)]
        score = scores_ref[...]
        top = jnp.maximum(score[:, :128], score[:, 128:])
        for shift in (8, 4, 2, 1):
            other = jnp.where(
                lane_all % (2 * shift) < shift,
                pltpu.roll(top, 128 - shift, 1),
                pltpu.roll(top, shift, 1),
            )
            top = jnp.maximum(top, other)
        weight = jnp.exp(score - jnp.concatenate([top, top], axis=1))
        w_high, w_low = parts_of(weight)
        pieces = []
        for g in range(12):
            v_high, v_low = spread(vals, g)
            wide = jnp.concatenate([v_high, ones], axis=1)
            rows = slice(32 * g, 32 * g + 32)
            both = dot(jnp.concatenate([w_high[rows], w_low[rows]], axis=0), wide)
            total = both[:32] + both[32:]
            mixed = total[:, :128] + dot(w_high[rows], v_low)
            pieces.append(mixed / total[:, 128:])
        attended.append(
            jnp.concatenate([p[:16] for p in pieces] + [p[16:] for p in pieces], axis=0)
        )
    attended = jnp.concatenate(attended, axis=1)
    by_member(sent_ref, dot3(parts_of(attended), parts_of(wout_ref[...])))


def gauss(x):
    z = jnp.clip(x * 0.7071067811865476, -3.832506856900711, 3.832506856900711)
    s = z * z
    top = 0.00022905065861350646
    for c in (0.0034082910107109506, 0.050955695062380861, 0.18520832239976145, 1.128379143519084):
        top = top * s + c
    low = -1.1791602954361697e-7
    for c in (
        0.000023547966471313185,
        0.0010179625278914885,
        0.014070470171167667,
        0.11098505178285362,
        0.49746925110067538,
        1.0,
    ):
        low = low * s + c
    return 0.5 + 0.5 * (z * top / low), 0.3989422804014327 * jnp.exp(-0.5 * (x * x))


def branch_kernel(
    first_ref, ret_ref, cot_ref, up_ref, down_ref,
    out_ref, mid_grad_ref, keep_ref, send_ref,
    mid_ref, normed_ref, scale_ref, nt_ref, cot_ref3, ct_ref, grad_up_ref, grad_down_ref,
):
    step = pl.program_id(0)

    @pl.when(step == 0)
    def _():
        mid = by_unit(first_ref) + by_unit(ret_ref)
        normed, scale = normalise(mid)
        mid_ref[...] = mid
        normed_ref[...] = normed
        scale_ref[...] = jnp.broadcast_to(scale, scale_ref.shape)
        n_high, n_low = parts_of(normed.T)
        nt_ref[0], nt_ref[1] = n_high, n_low
        cot = cot_ref[...]
        cot_ref3[0], cot_ref3[1] = parts_of(cot)
        ct_ref[0], ct_ref[1] = parts_of(cot.T)

    cot = (cot_ref3[0], cot_ref3[1])
    up = parts_of(up_ref[...])
    down = parts_of(down_ref[...])
    hidden = dot3(parts_of(normed_ref[...]), up)
    chance, density = gauss(hidden)
    active = parts_of(hidden * chance)
    d_hidden = parts_of(dot3(cot, down, NT) * (chance + hidden * density))
    cols = pl.ds(pl.multiple_of(step * HALF, HALF), HALF)
    grad_down_ref[:, cols] = dot3((ct_ref[0], ct_ref[1]), active)
    grad_up_ref[:, cols] = dot3((nt_ref[0], nt_ref[1]), d_hidden)
    out_part = dot3(active, down)
    norm_part = dot3(d_hidden, up, NT)

    @pl.when(step == 0)
    def _():
        out_ref[...] = mid_ref[...] + out_part
        mid_grad_ref[...] = norm_part

    @pl.when(step == 1)
    def _():
        out_ref[...] += out_part
        d_normed = mid_grad_ref[...] + norm_part
        normed = normed_ref[...]
        shift = jnp.mean(d_normed, axis=-1, keepdims=True)
        slope = jnp.mean(d_normed * normed, axis=-1, keepdims=True)
        mid_grad_ref[...] = cot_ref[...] + scale_ref[:, :1] * (d_normed - shift - normed * slope)
        pack(grad_up_ref, grad_down_ref, keep_ref, send_ref)


def pack(grad_up_ref, grad_down_ref, keep_ref, send_ref):
    core = lax.axis_index("c")
    lane = lax.broadcasted_iota(jnp.int32, (8, 128), 1)
    left = lane < 64
    segment = lane // 32
    first_core = jnp.full((72, 128), core, jnp.int32) == 0

    def piece(quarter, sigma, b):
        g, beta = b // 2, b % 2
        row = pl.multiple_of((4 * quarter + sigma) * 24, 8)

        def up_tile(i, t):
            return grad_up_ref[pl.ds(row + 8 * i, 8), 384 * g + 128 * t : 384 * g + 128 * (t + 1)]

        def down_tile(i, t):
            col = pl.multiple_of(384 * quarter + 128 * t, 128)
            return grad_down_ref[48 * b + 8 * i : 48 * b + 8 * (i + 1), pl.ds(col, 128)]

        full = [up_tile(i, 2 * beta) for i in range(3)]
        m0, m1, m2 = [up_tile(i, 1) for i in range(3)]
        own = left if beta == 0 else jnp.logical_not(left)
        if sigma == 0:
            c = [down_tile(i, 0) for i in range(6)]
        elif sigma == 1:
            c = [jnp.where(segment == 3, down_tile(i, 0), down_tile(i, 1)) for i in range(6)]
        elif sigma == 2:
            c = [jnp.where(segment == 0, down_tile(i, 2), down_tile(i, 1)) for i in range(6)]
        else:
            c = [down_tile(i, 2) for i in range(6)]
        free = 3 - sigma
        hole = segment == free
        start = 2 if beta == 0 else 0
        turn = 32 * ((start - (free + 2)) % 4)
        extra = pltpu.roll(c[4], turn, 1) if turn else c[4]
        rows = full + [
            jnp.where(own, m0, pltpu.roll(m1, 64, 1)),
            jnp.where(own, m2, extra),
            jnp.where(hole, pltpu.roll(c[5], 96, 1), c[0]),
            jnp.where(hole, pltpu.roll(c[5], 64, 1), c[1]),
            jnp.where(hole, pltpu.roll(c[5], 32, 1), c[2]),
            jnp.where(hole, pltpu.roll(c[4], 96, 1), c[3]),
        ]
        return jnp.concatenate(rows, axis=0)

    def quarter_body(quarter, carry):
        for pair in range(2):
            for b in range(8):
                even = piece(quarter, 2 * pair, b)
                odd = piece(quarter, 2 * pair + 1, b)
                where = (2 * quarter + pair) * 8 + b
                keep_ref[where] = jnp.where(first_core, even, odd)
                send_ref[where] = jnp.where(first_core, odd, even)
        return carry

    lax.fori_loop(0, 4, quarter_body, 0)


def finish_kernel(pieces_ref, up_ref, down_ref):
    scale = (TOK * 128) ** -0.5
    z = pieces_ref[0]
    for i in range(1, 64):
        z = z + pieces_ref[i]
    z = z * scale
    beta = lax.axis_index("zl")
    sigma = 2 * lax.axis_index("zh") + lax.axis_index("c")
    lane = lax.broadcasted_iota(jnp.int32, (8, 128), 1)
    lane24 = lax.broadcasted_iota(jnp.int32, (24, 128), 1)
    even24 = jnp.full((24, 128), beta, jnp.int32) == 0
    even = jnp.full((8, 128), beta, jnp.int32) == 0
    full, a, b = z[:24], z[24:32], z[32:40]
    turned = pltpu.roll(a, 64, 1)
    half = jnp.concatenate(
        [
            jnp.where(even, a, turned),
            jnp.where(even, turned, a),
            jnp.where(even, b, pltpu.roll(b, 64, 1)),
        ],
        axis=0,
    )
    swapped = pltpu.roll(full, 64, 1)
    up_ref[:, :128] = jnp.where(even24, full, jnp.where(lane24 < 64, half, swapped))
    up_ref[:, 128:] = jnp.where(even24, half, swapped)[:, :64]
    rest = z[40:]
    turned_rest = rest
    for k in range(1, 4):
        chosen = jnp.full((32, 128), sigma, jnp.int32) == k
        turned_rest = jnp.where(chosen, pltpu.roll(rest, 32 * k, 1), turned_rest)
    p0, p1, p2, p3 = [turned_rest[8 * i : 8 * (i + 1)] for i in range(4)]
    segment = lane // 32
    c5 = jnp.where(
        segment == 0,
        pltpu.roll(p0, 32, 1),
        jnp.where(segment == 1, pltpu.roll(p1, 64, 1), pltpu.roll(p2, 96, 1)),
    )
    tail = jnp.where(even, pltpu.roll(b, 96, 1), pltpu.roll(b, 32, 1))
    c4 = jnp.where(segment == 0, pltpu.roll(p3, 32, 1), tail)
    square = jnp.concatenate([p0, p1, p2, p3, c4, c5, jnp.zeros((80, 128), F32)], axis=0)
    down_ref[...] = square.T[:96, :48]


def shape(*dims):
    return jax.ShapeDtypeStruct(dims, F32)


def on_device(tokens, nbr_offset, cotangent, conv_weight, w_qkv, w_out, score_bias, w_up, w_down):
    local = tokens[0]
    forward = [(i, i + 1) for i in range(SCENE - 1)]
    backward = [(target, source) for source, target in forward]
    low = lax.ppermute(local[TOK - HALO :], SCENE_AXES, forward)
    high = lax.ppermute(local[:HALO], SCENE_AXES, backward)
    bias = score_bias.reshape(3, 8, 16, 2, 16, 2).transpose(3, 2, 0, 5, 1, 4).reshape(32, 768)

    sent = pl.pallas_call(
        conv_kernel,
        out_shape=shape(3 * TOK, 128),
        in_specs=[VMEM_SPEC] * 5,
        out_specs=VMEM_SPEC,
        compiler_params=PARAMS,
        name="conv",
    )(local, low, high, nbr_offset, conv_weight)

    def exchange(values):
        swapped = lax.all_to_all(
            values.reshape(SCENE, 3 * UNITS, 128), SCENE_AXES, split_axis=0, concat_axis=0, tiled=True
        )
        return swapped.reshape(3 * TOK, 128)

    mixed = pl.pallas_call(
        attention_kernel,
        out_shape=shape(3 * TOK, 128),
        in_specs=[VMEM_SPEC] * 4,
        out_specs=VMEM_SPEC,
        scratch_shapes=[pltpu.VMEM((TOK, 256), F32)],
        compiler_params=PARAMS,
        name="attention",
    )(exchange(sent), w_qkv, w_out, bias)
    returned = exchange(mixed)

    whole = lambda *dims: pl.BlockSpec(dims, lambda n: (0,) * len(dims))
    block_out, grad_mid, keep, send = pl.pallas_call(
        branch_kernel,
        grid=(2,),
        out_shape=(shape(TOK, D), shape(TOK, D), shape(64, 72, 128), shape(64, 72, 128)),
        in_specs=[
            whole(3 * TOK, 128),
            whole(3 * TOK, 128),
            whole(TOK, D),
            pl.BlockSpec((D, HALF), lambda n: (0, n)),
            pl.BlockSpec((HALF, D), lambda n: (n, 0)),
        ],
        out_specs=(whole(TOK, D), whole(TOK, D), whole(64, 72, 128), whole(64, 72, 128)),
        scratch_shapes=[
            pltpu.VMEM((TOK, D), F32),
            pltpu.VMEM((TOK, D), F32),
            pltpu.VMEM((TOK, 128), F32),
            pltpu.VMEM((2, D, TOK), BF16),
            pltpu.VMEM((2, TOK, D), BF16),
            pltpu.VMEM((2, D, TOK), BF16),
            pltpu.VMEM((D, FF), F32),
            pltpu.VMEM((D, FF), F32),
        ],
        compiler_params=PARAMS,
        name="branch",
    )(sent, returned, cotangent[0], w_up, w_down)

    got = lax.ppermute(send, "c", [(0, 1), (1, 0)])
    pieces = lax.all_to_all(keep + got, CHIP_AXES, split_axis=0, concat_axis=0, tiled=True)
    grad_up, grad_down = pl.pallas_call(
        finish_kernel,
        out_shape=(shape(24, 192), shape(96, 48)),
        in_specs=[VMEM_SPEC],
        out_specs=(VMEM_SPEC, VMEM_SPEC),
        compiler_params=PARAMS,
        name="finish",
    )(pieces)
    return block_out[None], grad_mid[None], grad_up, grad_down


def solution(mesh):
    fine = Mesh(mesh.devices.reshape(4, 2, 2, 4, 2), (*SCENE_AXES, *BATCH_AXES))
    slab = P(BATCH_AXES, SCENE_AXES, None)
    shard = P(SCENE_AXES, BATCH_AXES)
    return jax.shard_map(
        on_device,
        mesh=fine,
        in_specs=(slab, P(None, BATCH_AXES, SCENE_AXES), slab, P(), P(), P(), P(), P(), P()),
        out_specs=(slab, slab, shard, shard),
        check_vma=False,
    )
```

```python
import functools

import jax
import jax.numpy as jnp
from jax import lax
from jax.experimental import pallas as pl
from jax.experimental.pallas import tpu as pltpu
from jax.sharding import Mesh
from jax.sharding import PartitionSpec as P

D = 384
FF = 1536
TAPS = 27
HALO = 64
TOK = 384
SCENE = 16
UNITS = 24
HALF = FF // 2
SCENE_AXES = ("y", "zh", "c")
BATCH_AXES = ("x", "zl")
YZ_AXES = ("y", "zh", "zl")
F32 = jnp.float32
BF16 = jnp.bfloat16
NN = (((1,), (0,)), ((), ()))
NT = (((1,), (1,)), ((), ()))
VMEM_SPEC = pl.BlockSpec(memory_space=pltpu.VMEM)
SUB = 256


def params(mebibytes):
    return pltpu.CompilerParams(vmem_limit_bytes=mebibytes * 1024 * 1024)


def cost(flops, moved):
    return pl.CostEstimate(flops=int(flops), bytes_accessed=int(moved), transcendentals=0)


def parts_of(values):
    high = values.astype(BF16)
    return high, (values - high.astype(F32)).astype(BF16)


def dot(a, b, dims=NN):
    return lax.dot_general(a, b, dims, preferred_element_type=F32)


def dot3(a, b, dims=NN):
    return dot(a[0], b[0], dims) + (dot(a[0], b[1], dims) + dot(a[1], b[0], dims))


def stack(values):
    return jnp.concatenate(parts_of(values), axis=0)


def dot_stacked(a, b, dims=NN):
    rows = a.shape[0] // 2
    both = dot(a, b[0], dims)
    return both[:rows] + (both[rows:] + dot(a[:rows], b[1], dims))


def normalise(values):
    average = jnp.mean(values, axis=-1, keepdims=True)
    centered = values - average
    variance = jnp.mean(centered * centered, axis=-1, keepdims=True)
    scale = lax.rsqrt(variance + 1e-05)
    return centered * scale, scale


def slots():
    return [2 * j + k for k in range(2) for j in range(12)]


def from_members(ref):
    rows = []
    for place in slots():
        tiles = [ref[pl.ds(UNITS * t + place, SCENE, stride=3 * UNITS), :] for t in range(3)]
        rows.append(jnp.concatenate(tiles, axis=1))
    return jnp.concatenate(rows, axis=0)


def to_members(ref, values):
    for unit, place in enumerate(slots()):
        for t in range(3):
            ref[pl.ds(UNITS * t + place, SCENE, stride=3 * UNITS), :] = values[
                SCENE * unit : SCENE * (unit + 1), 128 * t : 128 * (t + 1)
            ]


def convolve(tok, ext, offsets, weight_ref):
    middle_tap = TAPS // 2
    taps = [a for a in range(TAPS) if a != middle_tap]
    chunk = 13
    row = lax.broadcasted_iota(jnp.int32, (128, 32), 0)
    lanes = lax.broadcasted_iota(jnp.int32, (128, 256), 1)
    table = jnp.concatenate(parts_of(ext), axis=1)
    index = jnp.where(offsets > HALO, -1, offsets + row + HALO)
    acc = tok + tok * weight_ref[middle_tap : middle_tap + 1, :]
    for start in range(0, len(taps), chunk):
        hits = [
            jnp.where(index[:, a : a + 1] == lanes, 1.0, 0.0).astype(BF16)
            for a in taps[start : start + chunk]
        ]
        picked = dot(jnp.concatenate(hits, axis=0), table)
        for i, a in enumerate(taps[start : start + chunk]):
            piece = picked[128 * i : 128 * (i + 1)]
            acc = acc + (piece[:, :D] + piece[:, D:]) * weight_ref[a : a + 1, :]
    return acc


def offsets_of(nbr_ref, block):
    rows = nbr_ref[:, 0, 128 * block : 128 * (block + 1)]
    return jnp.concatenate([rows, jnp.zeros((5, 128), jnp.int32)], axis=0).T


def inner_kernel(tok_ref, nbr_ref, weight_ref, out_ref):
    out_ref[...] = convolve(
        tok_ref[128:256, :], tok_ref[64:320, :], offsets_of(nbr_ref, 1), weight_ref
    )


def edge_kernel(tok_ref, mate_ref, other_ref, nbr_ref, weight_ref, inner_ref, sent_ref):
    even = jnp.full((HALO, D), lax.axis_index("c"), jnp.int32) == 0
    low = jnp.where(even, other_ref[...], mate_ref[...])
    high = jnp.where(even, mate_ref[...], other_ref[...])
    head = convolve(
        tok_ref[:128, :],
        jnp.concatenate([low, tok_ref[:192, :]], axis=0),
        offsets_of(nbr_ref, 0),
        weight_ref,
    )
    tail = convolve(
        tok_ref[256:, :],
        jnp.concatenate([tok_ref[192:, :], high], axis=0),
        offsets_of(nbr_ref, 2),
        weight_ref,
    )
    to_members(sent_ref, jnp.concatenate([head, inner_ref[...], tail], axis=0))


def attention_kernel(got_ref, qkv_ref, wout_ref, bias_ref, sent_ref, rows_ref, scores_ref):
    for place in range(UNITS):
        group, half = place // 2, place % 2
        for t in range(3):
            rows_ref[pl.ds(TOK * t + 32 * group + half, SCENE, stride=2), :] = got_ref[
                pl.ds(UNITS * t + place, SCENE, stride=3 * UNITS), :
            ]
    normed, _ = normalise(
        jnp.concatenate([rows_ref[TOK * t : TOK * (t + 1), :] for t in range(3)], axis=1)
    )
    qkv = dot_stacked(stack(normed), parts_of(qkv_ref[...]))
    head_of = lax.broadcasted_iota(jnp.int32, (16, 128), 1) // 16
    row_head = (lax.broadcasted_iota(jnp.int32, (256, 128), 0) // 16) % 8
    ones = jnp.where(
        row_head == lax.broadcasted_iota(jnp.int32, (256, 128), 1) // 16, 1.0, 0.0
    ).astype(BF16)
    lane_all = lax.broadcasted_iota(jnp.int32, (TOK, 128), 1)

    def spread(values, group):
        pieces = []
        for half in range(2):
            piece = values[32 * group + 16 * half : 32 * group + 16 * half + 16]
            pieces += [jnp.where(head_of == h, piece, 0.0) for h in range(8)]
        return parts_of(jnp.concatenate(pieces, axis=0))

    attended = []
    for t in range(3):
        cols = slice(128 * t, 128 * (t + 1))
        query = qkv[:, :D][:, cols] * 0.25
        keys = qkv[:, D : 2 * D][:, cols]
        vals = qkv[:, 2 * D :][:, cols]
        bias = jnp.concatenate(
            [bias_ref[8 * t + h][:, 16 * half : 16 * half + 16] for half in range(2) for h in range(8)],
            axis=1,
        )
        for g in range(12):
            rows = slice(32 * g, 32 * g + 32)
            scores_ref[rows, :] = dot_stacked(stack(query[rows]), spread(keys, g), NT) + bias
        score = scores_ref[...]
        top = jnp.maximum(score[:, :128], score[:, 128:])
        for shift in (8, 4, 2, 1):
            other = jnp.where(
                lane_all % (2 * shift) < shift,
                pltpu.roll(top, 128 - shift, 1),
                pltpu.roll(top, shift, 1),
            )
            top = jnp.maximum(top, other)
        weight = jnp.exp(score - jnp.concatenate([top, top], axis=1))
        w_high, w_low = parts_of(weight)
        pieces = []
        for g in range(12):
            v_high, v_low = spread(vals, g)
            wide = jnp.concatenate([v_high, ones], axis=1)
            rows = slice(32 * g, 32 * g + 32)
            both = dot(jnp.concatenate([w_high[rows], w_low[rows]], axis=0), wide)
            total = both[:32] + both[32:]
            mixed = total[:, :128] + dot(w_high[rows], v_low)
            pieces.append(mixed / total[:, 128:])
        attended.append(jnp.concatenate(pieces, axis=0))
    attended = jnp.concatenate(attended, axis=1)
    mixed = dot_stacked(stack(attended), parts_of(wout_ref[...]))
    for t in range(3):
        rows_ref[TOK * t : TOK * (t + 1), :] = mixed[:, 128 * t : 128 * (t + 1)]
    for place in range(UNITS):
        group, half = place // 2, place % 2
        for t in range(3):
            sent_ref[pl.ds(UNITS * t + place, SCENE, stride=3 * UNITS), :] = rows_ref[
                pl.ds(TOK * t + 32 * group + half, SCENE, stride=2), :
            ]


def gauss(x):
    z = jnp.clip(x * 0.7071067811865476, -3.832506856900711, 3.832506856900711)
    s = z * z
    top = 0.00022905065861350646
    for c in (0.0034082910107109506, 0.050955695062380861, 0.18520832239976145, 1.128379143519084):
        top = top * s + c
    low = -1.1791602954361697e-7
    for c in (
        0.000023547966471313185,
        0.0010179625278914885,
        0.014070470171167667,
        0.11098505178285362,
        0.49746925110067538,
        1.0,
    ):
        low = low * s + c
    return 0.5 + 0.5 * (z * top / low), 0.3989422804014327 * jnp.exp(-0.5 * (x * x))


def gradient_kernel(
    first_ref, ret_ref, cot_ref, up_ref, down_ref,
    mid_ref, act_ref, dh_ref, keep_ref, send_ref,
    normed_ref, nt_ref, cot_pair_ref, ct_ref, grad_up_ref, grad_down_ref,
):
    step = pl.program_id(0)

    @pl.when(step == 0)
    def _():
        mid = from_members(first_ref) + from_members(ret_ref)
        mid_ref[...] = mid
        normed, _ = normalise(mid)
        cot = cot_ref[...]
        normed_ref[...] = stack(normed)
        nt_ref[...] = stack(normed.T)
        cot_pair_ref[...] = stack(cot)
        ct_ref[...] = stack(cot.T)

    def enter(i):
        cols = slice(SUB * i, SUB * (i + 1))
        hidden = dot_stacked(normed_ref[...], parts_of(up_ref[:, cols]))
        return hidden, dot_stacked(cot_pair_ref[...], parts_of(down_ref[cols, :]), NT)

    count = HALF // SUB
    ahead = enter(0)
    for i in range(count):
        hidden, d_active = ahead
        if i + 1 < count:
            ahead = enter(i + 1)
        chance, density = gauss(hidden)
        active = parts_of(hidden * chance)
        d_hidden = parts_of(d_active * (chance + hidden * density))
        here = slice(SUB * i, SUB * (i + 1))
        act_ref[:TOK, here], act_ref[TOK:, here] = active
        dh_ref[:TOK, here], dh_ref[TOK:, here] = d_hidden
        cols = pl.ds(pl.multiple_of(step * HALF + SUB * i, SUB), SUB)
        grad_down_ref[:, cols] = dot_stacked(ct_ref[...], active)
        grad_up_ref[:, cols] = dot_stacked(nt_ref[...], d_hidden)

    @pl.when(step == 1)
    def _():
        pack(grad_up_ref, grad_down_ref, keep_ref, send_ref)


def output_kernel(mid_ref, cot_ref, act_ref, dh_ref, up_ref, down_ref, out_ref, mid_grad_ref):
    step = pl.program_id(0)
    out_part = dot_stacked(act_ref[...], parts_of(down_ref[...]))
    norm_part = dot_stacked(dh_ref[...], parts_of(up_ref[...]), NT)

    @pl.when(step == 0)
    def _():
        out_ref[...] = mid_ref[...] + out_part
        mid_grad_ref[...] = norm_part

    @pl.when(step > 0)
    def _():
        out_ref[...] += out_part
        mid_grad_ref[...] += norm_part

    @pl.when(step == pl.num_programs(0) - 1)
    def _():
        normed, scale = normalise(mid_ref[...])
        d_normed = mid_grad_ref[...]
        shift = jnp.mean(d_normed, axis=-1, keepdims=True)
        slope = jnp.mean(d_normed * normed, axis=-1, keepdims=True)
        mid_grad_ref[...] = cot_ref[...] + scale * (d_normed - shift - normed * slope)


def pack(grad_up_ref, grad_down_ref, keep_ref, send_ref):
    core = lax.axis_index("c")
    lane = lax.broadcasted_iota(jnp.int32, (8, 128), 1)
    left = lane < 64
    segment = lane // 32
    first_core = jnp.full((72, 128), core, jnp.int32) == 0

    def piece(quarter, sigma, b):
        g, beta = b // 2, b % 2
        row = pl.multiple_of((4 * quarter + sigma) * 24, 8)

        def up_tile(i, t):
            return grad_up_ref[pl.ds(row + 8 * i, 8), 384 * g + 128 * t : 384 * g + 128 * (t + 1)]

        def down_tile(i, t):
            col = pl.multiple_of(384 * quarter + 128 * t, 128)
            return grad_down_ref[48 * b + 8 * i : 48 * b + 8 * (i + 1), pl.ds(col, 128)]

        full = [up_tile(i, 2 * beta) for i in range(3)]
        m0, m1, m2 = [up_tile(i, 1) for i in range(3)]
        own = left if beta == 0 else jnp.logical_not(left)
        if sigma == 0:
            c = [down_tile(i, 0) for i in range(6)]
        elif sigma == 1:
            c = [jnp.where(segment == 3, down_tile(i, 0), down_tile(i, 1)) for i in range(6)]
        elif sigma == 2:
            c = [jnp.where(segment == 0, down_tile(i, 2), down_tile(i, 1)) for i in range(6)]
        else:
            c = [down_tile(i, 2) for i in range(6)]
        free = 3 - sigma
        hole = segment == free
        start = 2 if beta == 0 else 0
        turn = 32 * ((start - (free + 2)) % 4)
        extra = pltpu.roll(c[4], turn, 1) if turn else c[4]
        rows = full + [
            jnp.where(own, m0, pltpu.roll(m1, 64, 1)),
            jnp.where(own, m2, extra),
            jnp.where(hole, pltpu.roll(c[5], 96, 1), c[0]),
            jnp.where(hole, pltpu.roll(c[5], 64, 1), c[1]),
            jnp.where(hole, pltpu.roll(c[5], 32, 1), c[2]),
            jnp.where(hole, pltpu.roll(c[4], 96, 1), c[3]),
        ]
        return jnp.concatenate(rows, axis=0)

    def quarter_body(quarter, carry):
        for pair in range(2):
            for b in range(8):
                even = piece(quarter, 2 * pair, b)
                odd = piece(quarter, 2 * pair + 1, b)
                where = (2 * quarter + pair) * 8 + (b % 2) * 4 + b // 2
                keep_ref[where] = jnp.where(first_core, even, odd)
                send_ref[where] = jnp.where(first_core, odd, even)
        return carry

    lax.fori_loop(0, 4, quarter_body, 0)


def add_kernel(a_ref, b_ref, out_ref):
    out_ref[...] = a_ref[...] + b_ref[...]


def sum_kernel(pieces_ref, total_ref):
    total = pieces_ref[0]
    for i in range(1, 16):
        total = total + pieces_ref[i]
    total_ref[...] = total


def finish_kernel(pieces_ref, up_ref, down_ref):
    scale = (TOK * 128) ** -0.5
    z = (pieces_ref[0] + pieces_ref[1]) + (pieces_ref[2] + pieces_ref[3])
    z = z * scale
    beta = lax.axis_index("zl")
    sigma = 2 * lax.axis_index("zh") + lax.axis_index("c")
    lane = lax.broadcasted_iota(jnp.int32, (8, 128), 1)
    lane24 = lax.broadcasted_iota(jnp.int32, (24, 128), 1)
    even24 = jnp.full((24, 128), beta, jnp.int32) == 0
    even = jnp.full((8, 128), beta, jnp.int32) == 0
    full, a, b = z[:24], z[24:32], z[32:40]
    turned = pltpu.roll(a, 64, 1)
    half = jnp.concatenate(
        [
            jnp.where(even, a, turned),
            jnp.where(even, turned, a),
            jnp.where(even, b, pltpu.roll(b, 64, 1)),
        ],
        axis=0,
    )
    swapped = pltpu.roll(full, 64, 1)
    up_ref[:, :128] = jnp.where(even24, full, jnp.where(lane24 < 64, half, swapped))
    up_ref[:, 128:] = jnp.where(even24, half, swapped)[:, :64]
    rest = z[40:]
    turned_rest = rest
    for k in range(1, 4):
        chosen = jnp.full((32, 128), sigma, jnp.int32) == k
        turned_rest = jnp.where(chosen, pltpu.roll(rest, 32 * k, 1), turned_rest)
    p0, p1, p2, p3 = [turned_rest[8 * i : 8 * (i + 1)] for i in range(4)]
    segment = lane // 32
    c5 = jnp.where(
        segment == 0,
        pltpu.roll(p0, 32, 1),
        jnp.where(segment == 1, pltpu.roll(p1, 64, 1), pltpu.roll(p2, 96, 1)),
    )
    tail = jnp.where(even, pltpu.roll(b, 96, 1), pltpu.roll(b, 32, 1))
    c4 = jnp.where(segment == 0, pltpu.roll(p3, 32, 1), tail)
    down_ref[...] = jnp.concatenate([p0, p1, p2, p3, c4, c5], axis=0)[:, :96]


def shape(*dims):
    return jax.ShapeDtypeStruct(dims, F32)


def on_device(tokens, nbr_offset, cotangent, conv_weight, w_qkv, w_out, score_bias, w_up, w_down):
    local = tokens[0]
    mates = [(i, i ^ 1) for i in range(SCENE)]
    others = [(i, i + 1) for i in range(1, SCENE - 1, 2)]
    others += [(target, source) for source, target in others]
    even = lax.axis_index("c") == 0
    head, tail = local[:HALO], local[TOK - HALO :]
    other = lax.ppermute(jnp.where(even, head, tail), SCENE_AXES, others)
    mate = lax.ppermute(jnp.where(even, tail, head), SCENE_AXES, mates)

    inner = pl.pallas_call(
        inner_kernel,
        out_shape=shape(128, D),
        in_specs=[VMEM_SPEC] * 3,
        out_specs=VMEM_SPEC,
        compiler_params=params(16),
        cost_estimate=cost(3e9, 1e6),
        name="inner",
    )(local, nbr_offset, conv_weight)
    sent = pl.pallas_call(
        edge_kernel,
        out_shape=shape(3 * TOK, 128),
        in_specs=[VMEM_SPEC] * 6,
        out_specs=VMEM_SPEC,
        compiler_params=params(24),
        cost_estimate=cost(6e9, 2e6),
        name="edges",
    )(local, mate, other, nbr_offset, conv_weight, inner)

    def exchange(values):
        swapped = lax.all_to_all(
            values.reshape(SCENE, 3 * UNITS, 128), SCENE_AXES, split_axis=0, concat_axis=0, tiled=True
        )
        return swapped.reshape(3 * TOK, 128)

    mixed = pl.pallas_call(
        attention_kernel,
        out_shape=shape(3 * TOK, 128),
        in_specs=[VMEM_SPEC] * 4,
        out_specs=VMEM_SPEC,
        scratch_shapes=[pltpu.VMEM((3 * TOK, 128), F32), pltpu.VMEM((TOK, 256), F32)],
        compiler_params=params(24),
        cost_estimate=cost(8e9, 4e6),
        name="attention",
    )(exchange(sent), w_qkv, w_out, score_bias)
    returned = exchange(mixed)

    whole = lambda *dims: pl.BlockSpec(dims, lambda n: (0,) * len(dims))
    pair = jax.ShapeDtypeStruct((2 * TOK, FF), BF16)
    middle, active, d_hidden, keep, send = pl.pallas_call(
        gradient_kernel,
        grid=(2,),
        out_shape=(shape(TOK, D), pair, pair, shape(64, 72, 128), shape(64, 72, 128)),
        in_specs=[
            whole(3 * TOK, 128),
            whole(3 * TOK, 128),
            whole(TOK, D),
            pl.BlockSpec((D, HALF), lambda n: (0, n)),
            pl.BlockSpec((HALF, D), lambda n: (n, 0)),
        ],
        out_specs=(
            whole(TOK, D),
            pl.BlockSpec((2 * TOK, HALF), lambda n: (0, n)),
            pl.BlockSpec((2 * TOK, HALF), lambda n: (0, n)),
            whole(64, 72, 128),
            whole(64, 72, 128),
        ),
        scratch_shapes=[
            pltpu.VMEM((2 * TOK, D), BF16),
            pltpu.VMEM((2 * D, TOK), BF16),
            pltpu.VMEM((2 * TOK, D), BF16),
            pltpu.VMEM((2 * D, TOK), BF16),
            pltpu.VMEM((D, FF), F32),
            pltpu.VMEM((D, FF), F32),
        ],
        compiler_params=params(44),
        cost_estimate=cost(16e9, 16e6),
        name="gradient",
    )(sent, returned, cotangent[0], w_up, w_down)
    got = lax.ppermute(send, "c", [(0, 1), (1, 0)])

    block = FF // 4
    block_out, grad_mid = pl.pallas_call(
        output_kernel,
        grid=(4,),
        out_shape=(shape(TOK, D), shape(TOK, D)),
        in_specs=[
            whole(TOK, D),
            whole(TOK, D),
            pl.BlockSpec((2 * TOK, block), lambda n: (0, n)),
            pl.BlockSpec((2 * TOK, block), lambda n: (0, n)),
            pl.BlockSpec((D, block), lambda n: (0, n)),
            pl.BlockSpec((block, D), lambda n: (n, 0)),
        ],
        out_specs=(whole(TOK, D), whole(TOK, D)),
        compiler_params=params(24),
        cost_estimate=cost(6e9, 11e6),
        name="outputs",
    )(middle, cotangent[0], active, d_hidden, w_up, w_down)

    keep, block_out, grad_mid = lax.optimization_barrier((keep, block_out, grad_mid))
    piece = pl.BlockSpec((8, 72, 128), lambda n: (n, 0, 0))
    chip = pl.pallas_call(
        add_kernel,
        grid=(8,),
        out_shape=pltpu.HBM((64, 72, 128), F32),
        in_specs=[piece, piece],
        out_specs=piece,
        compiler_params=params(16),
        name="add",
    )(keep, got)

    def swap(values, axes, count, rows):
        return lax.all_to_all(
            values.reshape(count, rows, 128), axes, split_axis=0, concat_axis=0, tiled=True
        )

    total = pl.pallas_call(
        sum_kernel,
        out_shape=shape(288, 128),
        in_specs=[VMEM_SPEC],
        out_specs=VMEM_SPEC,
        compiler_params=params(8),
        name="sum",
    )(swap(chip, YZ_AXES, 16, 288))
    grad_up, grad_down = pl.pallas_call(
        finish_kernel,
        out_shape=(shape(24, 192), shape(48, 96)),
        in_specs=[VMEM_SPEC],
        out_specs=(VMEM_SPEC, VMEM_SPEC),
        compiler_params=params(8),
        name="finish",
    )(swap(total, "x", 4, 72))
    grad_down = grad_down.T
    return block_out[None], grad_mid[None], grad_up, grad_down


def solution(mesh):
    fine = Mesh(mesh.devices.reshape(4, 2, 2, 4, 2), (*SCENE_AXES, *BATCH_AXES))
    slab = P(BATCH_AXES, SCENE_AXES, None)
    shard = P(SCENE_AXES, BATCH_AXES)
    return jax.shard_map(
        on_device,
        mesh=fine,
        in_specs=(slab, P(None, BATCH_AXES, SCENE_AXES), slab, P(), P(), P(), P(), P(), P()),
        out_specs=(slab, slab, shard, shard),
        check_vma=False,
    )
```

```python
import functools

import jax
import jax.numpy as jnp
from jax import lax
from jax.experimental import pallas as pl
from jax.experimental.pallas import tpu as pltpu
from jax.sharding import Mesh
from jax.sharding import PartitionSpec as P

D = 384
FF = 1536
TAPS = 27
HALO = 64
TOK = 384
SCENE = 16
UNITS = 24
HALF = FF // 2
SCENE_AXES = ("y", "zh", "c")
BATCH_AXES = ("x", "zl")
CHIP_AXES = ("y", "zh", "x", "zl")
F32 = jnp.float32
BF16 = jnp.bfloat16
NN = (((1,), (0,)), ((), ()))
NT = (((1,), (1,)), ((), ()))
VMEM_SPEC = pl.BlockSpec(memory_space=pltpu.VMEM)
SUB = 256


def params(mebibytes):
    return pltpu.CompilerParams(vmem_limit_bytes=mebibytes * 1024 * 1024)


def cost(flops, moved):
    return pl.CostEstimate(flops=int(flops), bytes_accessed=int(moved), transcendentals=0)


def parts_of(values):
    high = values.astype(BF16)
    return high, (values - high.astype(F32)).astype(BF16)


def dot(a, b, dims=NN):
    return lax.dot_general(a, b, dims, preferred_element_type=F32)


def dot3(a, b, dims=NN):
    return dot(a[0], b[0], dims) + (dot(a[0], b[1], dims) + dot(a[1], b[0], dims))


def stack(values):
    return jnp.concatenate(parts_of(values), axis=0)


def dot_stacked(a, b, dims=NN):
    rows = a.shape[0] // 2
    both = dot(a, b[0], dims)
    return both[:rows] + (both[rows:] + dot(a[:rows], b[1], dims))


def normalise(values):
    average = jnp.mean(values, axis=-1, keepdims=True)
    centered = values - average
    variance = jnp.mean(centered * centered, axis=-1, keepdims=True)
    scale = lax.rsqrt(variance + 1e-05)
    return centered * scale, scale


def slots():
    return [2 * j + k for k in range(2) for j in range(12)]


def from_members(ref):
    rows = []
    for place in slots():
        tiles = [ref[pl.ds(UNITS * t + place, SCENE, stride=3 * UNITS), :] for t in range(3)]
        rows.append(jnp.concatenate(tiles, axis=1))
    return jnp.concatenate(rows, axis=0)


def to_members(ref, values):
    for unit, place in enumerate(slots()):
        for t in range(3):
            ref[pl.ds(UNITS * t + place, SCENE, stride=3 * UNITS), :] = values[
                SCENE * unit : SCENE * (unit + 1), 128 * t : 128 * (t + 1)
            ]


def convolve(tok, ext, offsets, weight_ref):
    middle_tap = TAPS // 2
    taps = [a for a in range(TAPS) if a != middle_tap]
    chunk = 13
    row = lax.broadcasted_iota(jnp.int32, (128, 32), 0)
    lanes = lax.broadcasted_iota(jnp.int32, (128, 256), 1)
    table = jnp.concatenate(parts_of(ext), axis=1)
    index = jnp.where(offsets > HALO, -1, offsets + row + HALO)
    acc = tok + tok * weight_ref[middle_tap : middle_tap + 1, :]
    for start in range(0, len(taps), chunk):
        hits = [
            jnp.where(index[:, a : a + 1] == lanes, 1.0, 0.0).astype(BF16)
            for a in taps[start : start + chunk]
        ]
        picked = dot(jnp.concatenate(hits, axis=0), table)
        for i, a in enumerate(taps[start : start + chunk]):
            piece = picked[128 * i : 128 * (i + 1)]
            acc = acc + (piece[:, :D] + piece[:, D:]) * weight_ref[a : a + 1, :]
    return acc


def offsets_of(nbr_ref, block):
    rows = nbr_ref[:, 0, 128 * block : 128 * (block + 1)]
    return jnp.concatenate([rows, jnp.zeros((5, 128), jnp.int32)], axis=0).T


def inner_kernel(tok_hbm, nbr_hbm, weight_hbm, out_ref, tok_ref, nbr_ref, weight_ref, done):
    copies = [
        pltpu.make_async_copy(tok_hbm.at[pl.ds(HALO, 2 * 128), :], tok_ref, done.at[0]),
        pltpu.make_async_copy(nbr_hbm, nbr_ref, done.at[1]),
        pltpu.make_async_copy(weight_hbm, weight_ref, done.at[2]),
    ]
    for copy in copies:
        copy.start()
    for copy in copies:
        copy.wait()
    out_ref[...] = convolve(
        tok_ref[HALO : HALO + 128, :], tok_ref[...], offsets_of(nbr_ref, 1), weight_ref
    )


def edge_kernel(tok_ref, mate_ref, other_ref, nbr_ref, weight_ref, inner_ref, sent_ref):
    even = jnp.full((HALO, D), lax.axis_index("c"), jnp.int32) == 0
    low = jnp.where(even, other_ref[...], mate_ref[...])
    high = jnp.where(even, mate_ref[...], other_ref[...])
    head = convolve(
        tok_ref[:128, :],
        jnp.concatenate([low, tok_ref[:192, :]], axis=0),
        offsets_of(nbr_ref, 0),
        weight_ref,
    )
    tail = convolve(
        tok_ref[256:, :],
        jnp.concatenate([tok_ref[192:, :], high], axis=0),
        offsets_of(nbr_ref, 2),
        weight_ref,
    )
    to_members(sent_ref, jnp.concatenate([head, inner_ref[...], tail], axis=0))


def attention_kernel(got_ref, qkv_ref, wout_ref, bias_ref, sent_ref, rows_ref, scores_ref):
    for place in range(UNITS):
        group, half = place // 2, place % 2
        for t in range(3):
            rows_ref[pl.ds(TOK * t + 32 * group + half, SCENE, stride=2), :] = got_ref[
                pl.ds(UNITS * t + place, SCENE, stride=3 * UNITS), :
            ]
    normed, _ = normalise(
        jnp.concatenate([rows_ref[TOK * t : TOK * (t + 1), :] for t in range(3)], axis=1)
    )
    qkv = dot_stacked(stack(normed), parts_of(qkv_ref[...]))
    head_of = lax.broadcasted_iota(jnp.int32, (16, 128), 1) // 16
    row_head = (lax.broadcasted_iota(jnp.int32, (256, 128), 0) // 16) % 8
    ones = jnp.where(
        row_head == lax.broadcasted_iota(jnp.int32, (256, 128), 1) // 16, 1.0, 0.0
    ).astype(BF16)
    lane_all = lax.broadcasted_iota(jnp.int32, (TOK, 128), 1)

    def spread(values, group):
        pieces = []
        for half in range(2):
            piece = values[32 * group + 16 * half : 32 * group + 16 * half + 16]
            pieces += [jnp.where(head_of == h, piece, 0.0) for h in range(8)]
        return parts_of(jnp.concatenate(pieces, axis=0))

    attended = []
    for t in range(3):
        cols = slice(128 * t, 128 * (t + 1))
        query = qkv[:, :D][:, cols] * 0.25
        keys = qkv[:, D : 2 * D][:, cols]
        vals = qkv[:, 2 * D :][:, cols]
        bias = jnp.concatenate(
            [bias_ref[8 * t + h][:, 16 * half : 16 * half + 16] for half in range(2) for h in range(8)],
            axis=1,
        )
        for g in range(12):
            rows = slice(32 * g, 32 * g + 32)
            scores_ref[rows, :] = dot_stacked(stack(query[rows]), spread(keys, g), NT) + bias
        score = scores_ref[...]
        top = jnp.maximum(score[:, :128], score[:, 128:])
        for shift in (8, 4, 2, 1):
            other = jnp.where(
                lane_all % (2 * shift) < shift,
                pltpu.roll(top, 128 - shift, 1),
                pltpu.roll(top, shift, 1),
            )
            top = jnp.maximum(top, other)
        weight = jnp.exp(score - jnp.concatenate([top, top], axis=1))
        w_high, w_low = parts_of(weight)
        pieces = []
        for g in range(12):
            v_high, v_low = spread(vals, g)
            wide = jnp.concatenate([v_high, ones], axis=1)
            rows = slice(32 * g, 32 * g + 32)
            both = dot(jnp.concatenate([w_high[rows], w_low[rows]], axis=0), wide)
            total = both[:32] + both[32:]
            mixed = total[:, :128] + dot(w_high[rows], v_low)
            pieces.append(mixed / total[:, 128:])
        attended.append(jnp.concatenate(pieces, axis=0))
    attended = jnp.concatenate(attended, axis=1)
    mixed = dot_stacked(stack(attended), parts_of(wout_ref[...]))
    for t in range(3):
        rows_ref[TOK * t : TOK * (t + 1), :] = mixed[:, 128 * t : 128 * (t + 1)]
    for place in range(UNITS):
        group, half = place // 2, place % 2
        for t in range(3):
            sent_ref[pl.ds(UNITS * t + place, SCENE, stride=3 * UNITS), :] = rows_ref[
                pl.ds(TOK * t + 32 * group + half, SCENE, stride=2), :
            ]


def gauss(x):
    z = jnp.clip(x * 0.7071067811865476, -3.832506856900711, 3.832506856900711)
    s = z * z
    top = 0.00022905065861350646
    for c in (0.0034082910107109506, 0.050955695062380861, 0.18520832239976145, 1.128379143519084):
        top = top * s + c
    low = -1.1791602954361697e-7
    for c in (
        0.000023547966471313185,
        0.0010179625278914885,
        0.014070470171167667,
        0.11098505178285362,
        0.49746925110067538,
        1.0,
    ):
        low = low * s + c
    return 0.5 + 0.5 * (z * top / low), 0.3989422804014327 * jnp.exp(-0.5 * (x * x))


def gradient_kernel(
    first_ref, ret_ref, cot_ref, up_ref, down_ref,
    mid_ref, act_ref, dh_ref, keep_ref, send_ref,
    normed_ref, nt_ref, cot_pair_ref, ct_ref, grad_up_ref, grad_down_ref,
):
    step = pl.program_id(0)

    @pl.when(step == 0)
    def _():
        mid = from_members(first_ref) + from_members(ret_ref)
        mid_ref[...] = mid
        normed, _ = normalise(mid)
        cot = cot_ref[...]
        normed_ref[...] = stack(normed)
        nt_ref[...] = stack(normed.T)
        cot_pair_ref[...] = stack(cot)
        ct_ref[...] = stack(cot.T)

    def enter(i):
        cols = slice(SUB * i, SUB * (i + 1))
        hidden = dot_stacked(normed_ref[...], parts_of(up_ref[:, cols]))
        return hidden, dot_stacked(cot_pair_ref[...], parts_of(down_ref[cols, :]), NT)

    count = HALF // SUB
    ahead = enter(0)
    for i in range(count):
        hidden, d_active = ahead
        if i + 1 < count:
            ahead = enter(i + 1)
        chance, density = gauss(hidden)
        active = parts_of(hidden * chance)
        d_hidden = parts_of(d_active * (chance + hidden * density))
        here = slice(SUB * i, SUB * (i + 1))
        act_ref[:TOK, here], act_ref[TOK:, here] = active
        dh_ref[:TOK, here], dh_ref[TOK:, here] = d_hidden
        cols = pl.ds(pl.multiple_of(step * HALF + SUB * i, SUB), SUB)
        grad_down_ref[:, cols] = dot_stacked(ct_ref[...], active)
        grad_up_ref[:, cols] = dot_stacked(nt_ref[...], d_hidden)

    @pl.when(step == 1)
    def _():
        pack(grad_up_ref, grad_down_ref, keep_ref, send_ref)


def output_kernel(mid_ref, cot_ref, act_ref, dh_ref, up_ref, down_ref, out_ref, mid_grad_ref):
    step = pl.program_id(0)
    out_part = dot_stacked(act_ref[...], parts_of(down_ref[...]))
    norm_part = dot_stacked(dh_ref[...], parts_of(up_ref[...]), NT)

    @pl.when(step == 0)
    def _():
        out_ref[...] = mid_ref[...] + out_part
        mid_grad_ref[...] = norm_part

    @pl.when(step > 0)
    def _():
        out_ref[...] += out_part
        mid_grad_ref[...] += norm_part

    @pl.when(step == pl.num_programs(0) - 1)
    def _():
        normed, scale = normalise(mid_ref[...])
        d_normed = mid_grad_ref[...]
        shift = jnp.mean(d_normed, axis=-1, keepdims=True)
        slope = jnp.mean(d_normed * normed, axis=-1, keepdims=True)
        mid_grad_ref[...] = cot_ref[...] + scale * (d_normed - shift - normed * slope)


def pack(grad_up_ref, grad_down_ref, keep_ref, send_ref):
    core = lax.axis_index("c")
    lane = lax.broadcasted_iota(jnp.int32, (8, 128), 1)
    left = lane < 64
    segment = lane // 32

    def piece(quarter, sigma, g, beta):
        row = pl.multiple_of((4 * quarter + sigma) * 24, 8)

        def up_tile(i, t):
            return grad_up_ref[pl.ds(row + 8 * i, 8), 384 * g + 128 * t : 384 * g + 128 * (t + 1)]

        def down_tile(i, t):
            col = pl.multiple_of(384 * quarter + 128 * t, 128)
            start = 96 * g + 48 * beta + 8 * i
            return grad_down_ref[start : start + 8, pl.ds(col, 128)]

        full = [up_tile(i, 2 * beta) for i in range(3)]
        m0, m1, m2 = [up_tile(i, 1) for i in range(3)]
        own = left if beta == 0 else jnp.logical_not(left)
        if sigma == 0:
            c = [down_tile(i, 0) for i in range(6)]
        elif sigma == 1:
            c = [jnp.where(segment == 3, down_tile(i, 0), down_tile(i, 1)) for i in range(6)]
        elif sigma == 2:
            c = [jnp.where(segment == 0, down_tile(i, 2), down_tile(i, 1)) for i in range(6)]
        else:
            c = [down_tile(i, 2) for i in range(6)]
        free = 3 - sigma
        hole = segment == free
        start = 2 if beta == 0 else 0
        turn = 32 * ((start - (free + 2)) % 4)
        extra = pltpu.roll(c[4], turn, 1) if turn else c[4]
        return full + [
            jnp.where(own, m0, pltpu.roll(m1, 64, 1)),
            jnp.where(own, m2, extra),
            jnp.where(hole, pltpu.roll(c[5], 96, 1), c[0]),
            jnp.where(hole, pltpu.roll(c[5], 64, 1), c[1]),
            jnp.where(hole, pltpu.roll(c[5], 32, 1), c[2]),
            jnp.where(hole, pltpu.roll(c[4], 96, 1), c[3]),
        ]

    def lay(even_ref, odd_ref):
        def body(quarter, carry):
            for g in range(4):
                for sigma in range(4):
                    for beta in range(2):
                        ref = odd_ref if sigma % 2 else even_ref
                        where = (2 * quarter + sigma // 2) * 8 + 2 * g + beta
                        for i, rows in enumerate(piece(quarter, sigma, g, beta)):
                            ref[where, 8 * i : 8 * (i + 1), :] = rows
            return carry

        lax.fori_loop(0, 4, body, 0)

    @pl.when(core == 0)
    def _():
        lay(keep_ref, send_ref)

    @pl.when(core == 1)
    def _():
        lay(send_ref, keep_ref)


def finish_kernel(pieces_ref, up_ref, down_ref):
    scale = (TOK * 128) ** -0.5
    sums = []
    for k in range(4):
        total = pieces_ref[16 * k]
        for i in range(1, 16):
            total = total + pieces_ref[16 * k + i]
        sums.append(total)
    z = (sums[0] + sums[1]) + (sums[2] + sums[3])
    z = z * scale
    beta = lax.axis_index("zl")
    sigma = 2 * lax.axis_index("zh") + lax.axis_index("c")
    lane = lax.broadcasted_iota(jnp.int32, (8, 128), 1)
    lane24 = lax.broadcasted_iota(jnp.int32, (24, 128), 1)
    even24 = jnp.full((24, 128), beta, jnp.int32) == 0
    even = jnp.full((8, 128), beta, jnp.int32) == 0
    full, a, b = z[:24], z[24:32], z[32:40]
    turned = pltpu.roll(a, 64, 1)
    half = jnp.concatenate(
        [
            jnp.where(even, a, turned),
            jnp.where(even, turned, a),
            jnp.where(even, b, pltpu.roll(b, 64, 1)),
        ],
        axis=0,
    )
    swapped = pltpu.roll(full, 64, 1)
    up_ref[:, :128] = jnp.where(even24, full, jnp.where(lane24 < 64, half, swapped))
    up_ref[:, 128:] = jnp.where(even24, half, swapped)[:, :64]
    rest = z[40:]
    turned_rest = rest
    for k in range(1, 4):
        chosen = jnp.full((32, 128), sigma, jnp.int32) == k
        turned_rest = jnp.where(chosen, pltpu.roll(rest, 32 * k, 1), turned_rest)
    p0, p1, p2, p3 = [turned_rest[8 * i : 8 * (i + 1)] for i in range(4)]
    segment = lane // 32
    c5 = jnp.where(
        segment == 0,
        pltpu.roll(p0, 32, 1),
        jnp.where(segment == 1, pltpu.roll(p1, 64, 1), pltpu.roll(p2, 96, 1)),
    )
    tail = jnp.where(even, pltpu.roll(b, 96, 1), pltpu.roll(b, 32, 1))
    c4 = jnp.where(segment == 0, pltpu.roll(p3, 32, 1), tail)
    down_ref[...] = jnp.concatenate([p0, p1, p2, p3, c4, c5], axis=0)[:, :96]


def shape(*dims):
    return jax.ShapeDtypeStruct(dims, F32)


def on_device(tokens, nbr_offset, cotangent, conv_weight, w_qkv, w_out, score_bias, w_up, w_down):
    local = tokens[0]
    mates = [(i, i ^ 1) for i in range(SCENE)]
    others = [(i, i + 1) for i in range(1, SCENE - 1, 2)]
    others += [(target, source) for source, target in others]
    even = lax.axis_index("c") == 0
    head, tail = local[:HALO], local[TOK - HALO :]
    other = lax.ppermute(jnp.where(even, head, tail), SCENE_AXES, others)
    mate = lax.ppermute(jnp.where(even, tail, head), SCENE_AXES, mates)

    inner = pl.pallas_call(
        inner_kernel,
        out_shape=shape(128, D),
        in_specs=[pl.BlockSpec(memory_space=pltpu.HBM)] * 3,
        out_specs=VMEM_SPEC,
        scratch_shapes=[
            pltpu.VMEM((2 * 128, D), F32),
            pltpu.VMEM((TAPS, 1, TOK), jnp.int32),
            pltpu.VMEM((TAPS, D), F32),
            pltpu.SemaphoreType.DMA((3,)),
        ],
        compiler_params=params(16),
        cost_estimate=cost(3e9, 1e6),
        name="inner",
    )(*(pltpu.with_memory_space_constraint(a, pltpu.HBM) for a in (local, nbr_offset, conv_weight)))
    sent = pl.pallas_call(
        edge_kernel,
        out_shape=shape(3 * TOK, 128),
        in_specs=[VMEM_SPEC] * 6,
        out_specs=VMEM_SPEC,
        compiler_params=params(24),
        cost_estimate=cost(6e9, 2e6),
        name="edges",
    )(local, mate, other, nbr_offset, conv_weight, inner)

    def exchange(values):
        swapped = lax.all_to_all(
            values.reshape(SCENE, 3 * UNITS, 128), SCENE_AXES, split_axis=0, concat_axis=0, tiled=True
        )
        return swapped.reshape(3 * TOK, 128)

    mixed = pl.pallas_call(
        attention_kernel,
        out_shape=shape(3 * TOK, 128),
        in_specs=[VMEM_SPEC] * 4,
        out_specs=VMEM_SPEC,
        scratch_shapes=[pltpu.VMEM((3 * TOK, 128), F32), pltpu.VMEM((TOK, 256), F32)],
        compiler_params=params(24),
        cost_estimate=cost(8e9, 4e6),
        name="attention",
    )(exchange(sent), w_qkv, w_out, score_bias)
    returned = exchange(mixed)

    whole = lambda *dims: pl.BlockSpec(dims, lambda n: (0,) * len(dims))
    pair = pltpu.HBM((2 * TOK, FF), BF16)
    middle, active, d_hidden, keep, send = pl.pallas_call(
        gradient_kernel,
        grid=(2,),
        out_shape=(shape(TOK, D), pair, pair, shape(64, 72, 128), shape(64, 72, 128)),
        in_specs=[
            whole(3 * TOK, 128),
            whole(3 * TOK, 128),
            whole(TOK, D),
            pl.BlockSpec((D, HALF), lambda n: (0, n)),
            pl.BlockSpec((HALF, D), lambda n: (n, 0)),
        ],
        out_specs=(
            whole(TOK, D),
            pl.BlockSpec((2 * TOK, HALF), lambda n: (0, n)),
            pl.BlockSpec((2 * TOK, HALF), lambda n: (0, n)),
            whole(64, 72, 128),
            whole(64, 72, 128),
        ),
        scratch_shapes=[
            pltpu.VMEM((2 * TOK, D), BF16),
            pltpu.VMEM((2 * D, TOK), BF16),
            pltpu.VMEM((2 * TOK, D), BF16),
            pltpu.VMEM((2 * D, TOK), BF16),
            pltpu.VMEM((D, FF), F32),
            pltpu.VMEM((D, FF), F32),
        ],
        compiler_params=params(44),
        cost_estimate=cost(16e9, 16e6),
        name="gradient",
    )(sent, returned, cotangent[0], w_up, w_down)
    got = lax.ppermute(send, "c", [(0, 1), (1, 0)])

    block = FF // 4
    block_out, grad_mid = pl.pallas_call(
        output_kernel,
        grid=(4,),
        out_shape=(shape(TOK, D), shape(TOK, D)),
        in_specs=[
            whole(TOK, D),
            whole(TOK, D),
            pl.BlockSpec((2 * TOK, block), lambda n: (0, n)),
            pl.BlockSpec((2 * TOK, block), lambda n: (0, n)),
            pl.BlockSpec((D, block), lambda n: (0, n)),
            pl.BlockSpec((block, D), lambda n: (n, 0)),
        ],
        out_specs=(whole(TOK, D), whole(TOK, D)),
        compiler_params=params(24),
        cost_estimate=cost(6e9, 11e6),
        name="outputs",
    )(middle, cotangent[0], active, d_hidden, w_up, w_down)

    pieces = lax.all_to_all(keep + got, CHIP_AXES, split_axis=0, concat_axis=0, tiled=True)
    grad_up, grad_down = pl.pallas_call(
        finish_kernel,
        out_shape=(shape(24, 192), shape(48, 96)),
        in_specs=[VMEM_SPEC],
        out_specs=(VMEM_SPEC, VMEM_SPEC),
        compiler_params=params(8),
        name="finish",
    )(pieces)
    grad_down = grad_down.T
    return block_out[None], grad_mid[None], grad_up, grad_down


def solution(mesh):
    fine = Mesh(mesh.devices.reshape(4, 2, 2, 4, 2), (*SCENE_AXES, *BATCH_AXES))
    slab = P(BATCH_AXES, SCENE_AXES, None)
    shard = P(SCENE_AXES, BATCH_AXES)
    return jax.shard_map(
        on_device,
        mesh=fine,
        in_specs=(slab, P(None, BATCH_AXES, SCENE_AXES), slab, P(), P(), P(), P(), P(), P()),
        out_specs=(slab, slab, shard, shard),
        check_vma=False,
    )
```

```python
import functools

import jax
import jax.numpy as jnp
from jax import lax
from jax.experimental import pallas as pl
from jax.experimental.pallas import tpu as pltpu
from jax.sharding import Mesh
from jax.sharding import PartitionSpec as P

D = 384
FF = 1536
TAPS = 27
HALO = 64
TOK = 384
SCENE = 16
UNITS = 24
SCENE_AXES = ("y", "zh", "c")
BATCH_AXES = ("x", "zl")
CHIP_AXES = ("y", "zh", "x", "zl")
F32 = jnp.float32
BF16 = jnp.bfloat16
NN = (((1,), (0,)), ((), ()))
NT = (((1,), (1,)), ((), ()))
VMEM_SPEC = pl.BlockSpec(memory_space=pltpu.VMEM)
SUB = 256


def params(mebibytes):
    return pltpu.CompilerParams(vmem_limit_bytes=mebibytes * 1024 * 1024)


def cost(flops, moved):
    return pl.CostEstimate(flops=int(flops), bytes_accessed=int(moved), transcendentals=0)


def parts_of(values):
    high = values.astype(BF16)
    return high, (values - high.astype(F32)).astype(BF16)


def dot(a, b, dims=NN):
    return lax.dot_general(a, b, dims, preferred_element_type=F32)


def dot3(a, b, dims=NN):
    return dot(a[0], b[0], dims) + (dot(a[0], b[1], dims) + dot(a[1], b[0], dims))


def stack(values):
    return jnp.concatenate(parts_of(values), axis=0)


def dot_stacked(a, b, dims=NN):
    rows = a.shape[0] // 2
    both = dot(a, b[0], dims)
    return both[:rows] + (both[rows:] + dot(a[:rows], b[1], dims))


def normalise(values):
    average = jnp.mean(values, axis=-1, keepdims=True)
    centered = values - average
    variance = jnp.mean(centered * centered, axis=-1, keepdims=True)
    scale = lax.rsqrt(variance + 1e-05)
    return centered * scale, scale


def slots():
    return [2 * j + k for k in range(2) for j in range(12)]


def from_members(ref):
    rows = []
    for place in slots():
        tiles = [ref[pl.ds(UNITS * t + place, SCENE, stride=3 * UNITS), :] for t in range(3)]
        rows.append(jnp.concatenate(tiles, axis=1))
    return jnp.concatenate(rows, axis=0)


def to_members(ref, values):
    for unit, place in enumerate(slots()):
        for t in range(3):
            ref[pl.ds(UNITS * t + place, SCENE, stride=3 * UNITS), :] = values[
                SCENE * unit : SCENE * (unit + 1), 128 * t : 128 * (t + 1)
            ]


def convolve(tok, ext, offsets, weight_ref):
    middle_tap = TAPS // 2
    taps = [a for a in range(TAPS) if a != middle_tap]
    chunk = 13
    count = tok.shape[0]
    row = lax.broadcasted_iota(jnp.int32, (count, 32), 0)
    lanes = lax.broadcasted_iota(jnp.int32, (count, ext.shape[0]), 1)
    table = jnp.concatenate(parts_of(ext), axis=1)
    index = jnp.where(offsets > HALO, -1, offsets + row + HALO)
    acc = tok + tok * weight_ref[middle_tap : middle_tap + 1, :]
    for start in range(0, len(taps), chunk):
        hits = [
            jnp.where(index[:, a : a + 1] == lanes, 1.0, 0.0).astype(BF16)
            for a in taps[start : start + chunk]
        ]
        picked = dot(jnp.concatenate(hits, axis=0), table)
        for i, a in enumerate(taps[start : start + chunk]):
            piece = picked[count * i : count * (i + 1)]
            acc = acc + (piece[:, :D] + piece[:, D:]) * weight_ref[a : a + 1, :]
    return acc


def offsets_of(nbr_ref):
    return jnp.concatenate([nbr_ref[:, 0, :], jnp.zeros((5, TOK), jnp.int32)], axis=0).T


def inner_kernel(tok_hbm, nbr_hbm, weight_hbm, out_ref, tok_ref, nbr_ref, weight_ref, done):
    copies = [
        pltpu.make_async_copy(tok_hbm, tok_ref, done.at[0]),
        pltpu.make_async_copy(nbr_hbm, nbr_ref, done.at[1]),
        pltpu.make_async_copy(weight_hbm, weight_ref, done.at[2]),
    ]
    for copy in copies:
        copy.start()
    for copy in copies:
        copy.wait()
    offsets = offsets_of(nbr_ref)
    for start in (HALO, HALO + 128):
        out_ref[start - HALO : start - HALO + 128, :] = convolve(
            tok_ref[start : start + 128, :],
            tok_ref[start - HALO : start + 128 + HALO, :],
            offsets[start : start + 128],
            weight_ref,
        )


def edge_kernel(tok_ref, mate_ref, other_ref, nbr_ref, weight_ref, inner_ref, sent_ref):
    even = jnp.full((HALO, D), lax.axis_index("c"), jnp.int32) == 0
    low = jnp.where(even, other_ref[...], mate_ref[...])
    high = jnp.where(even, mate_ref[...], other_ref[...])
    offsets = offsets_of(nbr_ref)
    blank = jnp.zeros((HALO, D), F32)
    head = convolve(
        tok_ref[:HALO, :],
        jnp.concatenate([low, tok_ref[: 2 * HALO, :], blank], axis=0),
        offsets[:HALO],
        weight_ref,
    )
    tail = convolve(
        tok_ref[TOK - HALO :, :],
        jnp.concatenate([tok_ref[TOK - 2 * HALO :, :], high, blank], axis=0),
        offsets[TOK - HALO :],
        weight_ref,
    )
    to_members(sent_ref, jnp.concatenate([head, inner_ref[...], tail], axis=0))


def attention_kernel(got_ref, qkv_ref, wout_ref, bias_ref, sent_ref, rows_ref, scores_ref):
    for place in range(UNITS):
        group, half = place // 2, place % 2
        for t in range(3):
            rows_ref[pl.ds(TOK * t + 32 * group + half, SCENE, stride=2), :] = got_ref[
                pl.ds(UNITS * t + place, SCENE, stride=3 * UNITS), :
            ]
    normed, _ = normalise(
        jnp.concatenate([rows_ref[TOK * t : TOK * (t + 1), :] for t in range(3)], axis=1)
    )
    qkv = dot_stacked(stack(normed), parts_of(qkv_ref[...]))
    head_of = lax.broadcasted_iota(jnp.int32, (16, 128), 1) // 16
    row_head = (lax.broadcasted_iota(jnp.int32, (256, 128), 0) // 16) % 8
    ones = jnp.where(
        row_head == lax.broadcasted_iota(jnp.int32, (256, 128), 1) // 16, 1.0, 0.0
    ).astype(BF16)
    lane_all = lax.broadcasted_iota(jnp.int32, (TOK, 128), 1)

    def spread(values, group):
        pieces = []
        for half in range(2):
            piece = values[32 * group + 16 * half : 32 * group + 16 * half + 16]
            pieces += [jnp.where(head_of == h, piece, 0.0) for h in range(8)]
        return parts_of(jnp.concatenate(pieces, axis=0))

    attended = []
    for t in range(3):
        cols = slice(128 * t, 128 * (t + 1))
        query = qkv[:, :D][:, cols] * 0.25
        keys = qkv[:, D : 2 * D][:, cols]
        vals = qkv[:, 2 * D :][:, cols]
        bias = jnp.concatenate(
            [bias_ref[8 * t + h][:, 16 * half : 16 * half + 16] for half in range(2) for h in range(8)],
            axis=1,
        )
        for g in range(12):
            rows = slice(32 * g, 32 * g + 32)
            scores_ref[rows, :] = dot_stacked(stack(query[rows]), spread(keys, g), NT) + bias
        score = scores_ref[...]
        top = jnp.maximum(score[:, :128], score[:, 128:])
        for shift in (8, 4, 2, 1):
            other = jnp.where(
                lane_all % (2 * shift) < shift,
                pltpu.roll(top, 128 - shift, 1),
                pltpu.roll(top, shift, 1),
            )
            top = jnp.maximum(top, other)
        weight = jnp.exp(score - jnp.concatenate([top, top], axis=1))
        w_high, w_low = parts_of(weight)
        pieces = []
        for g in range(12):
            v_high, v_low = spread(vals, g)
            wide = jnp.concatenate([v_high, ones], axis=1)
            rows = slice(32 * g, 32 * g + 32)
            both = dot(jnp.concatenate([w_high[rows], w_low[rows]], axis=0), wide)
            total = both[:32] + both[32:]
            mixed = total[:, :128] + dot(w_high[rows], v_low)
            pieces.append(mixed / total[:, 128:])
        attended.append(jnp.concatenate(pieces, axis=0))
    attended = jnp.concatenate(attended, axis=1)
    mixed = dot_stacked(stack(attended), parts_of(wout_ref[...]))
    for t in range(3):
        rows_ref[TOK * t : TOK * (t + 1), :] = mixed[:, 128 * t : 128 * (t + 1)]
    for place in range(UNITS):
        group, half = place // 2, place % 2
        for t in range(3):
            sent_ref[pl.ds(UNITS * t + place, SCENE, stride=3 * UNITS), :] = rows_ref[
                pl.ds(TOK * t + 32 * group + half, SCENE, stride=2), :
            ]


def gauss(x):
    z = jnp.clip(x * 0.7071067811865476, -3.832506856900711, 3.832506856900711)
    s = z * z
    top = 0.00022905065861350646
    for c in (0.0034082910107109506, 0.050955695062380861, 0.18520832239976145, 1.128379143519084):
        top = top * s + c
    low = -1.1791602954361697e-7
    for c in (
        0.000023547966471313185,
        0.0010179625278914885,
        0.014070470171167667,
        0.11098505178285362,
        0.49746925110067538,
        1.0,
    ):
        low = low * s + c
    return 0.5 + 0.5 * (z * top / low), 0.3989422804014327 * jnp.exp(-0.5 * (x * x))


def prepare_kernel(cot_ref, up_ref, down_ref, d_active_ref, up_high_ref, up_low_ref, ct_ref):
    @pl.when(pl.program_id(0) == 0)
    def _():
        ct_ref[...] = stack(cot_ref[...].T)

    d_active_ref[...] = dot_stacked(stack(cot_ref[...]), parts_of(down_ref[...]), NT)
    up_high_ref[...], up_low_ref[...] = parts_of(up_ref[...])


def gradient_kernel(
    first_ref, ret_ref, d_active_hbm, up_high_hbm, up_low_hbm, ct_hbm,
    mid_hbm, act_hbm, dh_hbm, keep_ref, send_ref,
    d_active_ref, up_high_ref, up_low_ref, ct_ref, mid_ref, act_ref, dh_ref,
    normed_ref, nt_ref, grad_up_ref, grad_down_ref, came, left,
):
    pairs = (
        (up_high_hbm, up_high_ref),
        (up_low_hbm, up_low_ref),
        (d_active_hbm, d_active_ref),
        (ct_hbm, ct_ref),
    )
    loads = [pltpu.make_async_copy(src, dst, came.at[i]) for i, (src, dst) in enumerate(pairs)]
    for load in loads:
        load.start()
    mid = from_members(first_ref) + from_members(ret_ref)
    mid_ref[...] = mid
    stores = [pltpu.make_async_copy(mid_ref, mid_hbm, left.at[0])]
    stores[0].start()
    normed, _ = normalise(mid)
    normed_ref[...] = stack(normed)
    nt_ref[...] = stack(normed.T)

    def enter(i):
        cols = slice(SUB * i, SUB * (i + 1))
        return dot_stacked(normed_ref[...], (up_high_ref[:, cols], up_low_ref[:, cols]))

    loads[0].wait()
    loads[1].wait()
    count = FF // SUB
    ahead = enter(0)
    loads[2].wait()
    loads[3].wait()
    for i in range(count):
        hidden = ahead
        if i + 1 < count:
            ahead = enter(i + 1)
        here = slice(SUB * i, SUB * (i + 1))
        chance, density = gauss(hidden)
        active = parts_of(hidden * chance)
        d_hidden = parts_of(d_active_ref[:, here] * (chance + hidden * density))
        act_ref[i, :TOK, :], act_ref[i, TOK:, :] = active
        dh_ref[i, :TOK, :], dh_ref[i, TOK:, :] = d_hidden
        grad_down_ref[:, here] = dot_stacked(ct_ref[...], active)
        grad_up_ref[:, here] = dot_stacked(nt_ref[...], d_hidden)
    stores.append(pltpu.make_async_copy(act_ref, act_hbm, left.at[1]))
    stores.append(pltpu.make_async_copy(dh_ref, dh_hbm, left.at[2]))
    stores[1].start()
    stores[2].start()
    pack(grad_up_ref, grad_down_ref, keep_ref, send_ref)
    for store in stores:
        store.wait()


def output_kernel(mid_ref, cot_ref, act_ref, dh_ref, up_ref, down_ref, out_ref, mid_grad_ref):
    step = pl.program_id(0)
    out_part = dot_stacked(act_ref[0], parts_of(down_ref[...]))
    norm_part = dot_stacked(dh_ref[0], parts_of(up_ref[...]), NT)

    @pl.when(step == 0)
    def _():
        out_ref[...] = mid_ref[...] + out_part
        mid_grad_ref[...] = norm_part

    @pl.when(step > 0)
    def _():
        out_ref[...] += out_part
        mid_grad_ref[...] += norm_part

    @pl.when(step == pl.num_programs(0) - 1)
    def _():
        normed, scale = normalise(mid_ref[...])
        d_normed = mid_grad_ref[...]
        shift = jnp.mean(d_normed, axis=-1, keepdims=True)
        slope = jnp.mean(d_normed * normed, axis=-1, keepdims=True)
        mid_grad_ref[...] = cot_ref[...] + scale * (d_normed - shift - normed * slope)


def pack(grad_up_ref, grad_down_ref, keep_ref, send_ref):
    core = lax.axis_index("c")
    lane = lax.broadcasted_iota(jnp.int32, (8, 128), 1)
    left = lane < 64
    segment = lane // 32

    def piece(quarter, sigma, g, beta):
        row = pl.multiple_of((4 * quarter + sigma) * 24, 8)

        def up_tile(i, t):
            return grad_up_ref[pl.ds(row + 8 * i, 8), 384 * g + 128 * t : 384 * g + 128 * (t + 1)]

        def down_tile(i, t):
            col = pl.multiple_of(384 * quarter + 128 * t, 128)
            start = 96 * g + 48 * beta + 8 * i
            return grad_down_ref[start : start + 8, pl.ds(col, 128)]

        full = [up_tile(i, 2 * beta) for i in range(3)]
        m0, m1, m2 = [up_tile(i, 1) for i in range(3)]
        own = left if beta == 0 else jnp.logical_not(left)
        if sigma == 0:
            c = [down_tile(i, 0) for i in range(6)]
        elif sigma == 1:
            c = [jnp.where(segment == 3, down_tile(i, 0), down_tile(i, 1)) for i in range(6)]
        elif sigma == 2:
            c = [jnp.where(segment == 0, down_tile(i, 2), down_tile(i, 1)) for i in range(6)]
        else:
            c = [down_tile(i, 2) for i in range(6)]
        free = 3 - sigma
        hole = segment == free
        start = 2 if beta == 0 else 0
        turn = 32 * ((start - (free + 2)) % 4)
        extra = pltpu.roll(c[4], turn, 1) if turn else c[4]
        return full + [
            jnp.where(own, m0, pltpu.roll(m1, 64, 1)),
            jnp.where(own, m2, extra),
            jnp.where(hole, pltpu.roll(c[5], 96, 1), c[0]),
            jnp.where(hole, pltpu.roll(c[5], 64, 1), c[1]),
            jnp.where(hole, pltpu.roll(c[5], 32, 1), c[2]),
            jnp.where(hole, pltpu.roll(c[4], 96, 1), c[3]),
        ]

    def lay(even_ref, odd_ref):
        def body(quarter, carry):
            for g in range(4):
                for sigma in range(4):
                    for beta in range(2):
                        ref = odd_ref if sigma % 2 else even_ref
                        where = (2 * quarter + sigma // 2) * 8 + 2 * g + beta
                        for i, rows in enumerate(piece(quarter, sigma, g, beta)):
                            ref[where, 8 * i : 8 * (i + 1), :] = rows
            return carry

        lax.fori_loop(0, 4, body, 0)

    @pl.when(core == 0)
    def _():
        lay(keep_ref, send_ref)

    @pl.when(core == 1)
    def _():
        lay(send_ref, keep_ref)


def finish_kernel(pieces_ref, up_ref, down_ref):
    scale = (TOK * 128) ** -0.5
    sums = []
    for k in range(4):
        total = pieces_ref[16 * k]
        for i in range(1, 16):
            total = total + pieces_ref[16 * k + i]
        sums.append(total)
    z = (sums[0] + sums[1]) + (sums[2] + sums[3])
    z = z * scale
    beta = lax.axis_index("zl")
    sigma = 2 * lax.axis_index("zh") + lax.axis_index("c")
    lane = lax.broadcasted_iota(jnp.int32, (8, 128), 1)
    lane24 = lax.broadcasted_iota(jnp.int32, (24, 128), 1)
    even24 = jnp.full((24, 128), beta, jnp.int32) == 0
    even = jnp.full((8, 128), beta, jnp.int32) == 0
    full, a, b = z[:24], z[24:32], z[32:40]
    turned = pltpu.roll(a, 64, 1)
    half = jnp.concatenate(
        [
            jnp.where(even, a, turned),
            jnp.where(even, turned, a),
            jnp.where(even, b, pltpu.roll(b, 64, 1)),
        ],
        axis=0,
    )
    swapped = pltpu.roll(full, 64, 1)
    up_ref[:, :128] = jnp.where(even24, full, jnp.where(lane24 < 64, half, swapped))
    up_ref[:, 128:] = jnp.where(even24, half, swapped)[:, :64]
    rest = z[40:]
    turned_rest = rest
    for k in range(1, 4):
        chosen = jnp.full((32, 128), sigma, jnp.int32) == k
        turned_rest = jnp.where(chosen, pltpu.roll(rest, 32 * k, 1), turned_rest)
    p0, p1, p2, p3 = [turned_rest[8 * i : 8 * (i + 1)] for i in range(4)]
    segment = lane // 32
    c5 = jnp.where(
        segment == 0,
        pltpu.roll(p0, 32, 1),
        jnp.where(segment == 1, pltpu.roll(p1, 64, 1), pltpu.roll(p2, 96, 1)),
    )
    tail = jnp.where(even, pltpu.roll(b, 96, 1), pltpu.roll(b, 32, 1))
    c4 = jnp.where(segment == 0, pltpu.roll(p3, 32, 1), tail)
    down_ref[...] = jnp.concatenate([p0, p1, p2, p3, c4, c5], axis=0)[:, :96]


def shape(*dims):
    return jax.ShapeDtypeStruct(dims, F32)


def on_device(tokens, nbr_offset, cotangent, conv_weight, w_qkv, w_out, score_bias, w_up, w_down):
    local = tokens[0]
    mates = [(i, i ^ 1) for i in range(SCENE)]
    others = [(i, i + 1) for i in range(1, SCENE - 1, 2)]
    others += [(target, source) for source, target in others]
    even = lax.axis_index("c") == 0
    head, tail = local[:HALO], local[TOK - HALO :]
    other = lax.ppermute(jnp.where(even, head, tail), SCENE_AXES, others)
    mate = lax.ppermute(jnp.where(even, tail, head), SCENE_AXES, mates)

    inner = pl.pallas_call(
        inner_kernel,
        out_shape=shape(256, D),
        in_specs=[pl.BlockSpec(memory_space=pltpu.HBM)] * 3,
        out_specs=VMEM_SPEC,
        scratch_shapes=[
            pltpu.VMEM((TOK, D), F32),
            pltpu.VMEM((TAPS, 1, TOK), jnp.int32),
            pltpu.VMEM((TAPS, D), F32),
            pltpu.SemaphoreType.DMA((3,)),
        ],
        compiler_params=params(16),
        cost_estimate=cost(3e9, 1e6),
        name="inner",
    )(*(pltpu.with_memory_space_constraint(a, pltpu.HBM) for a in (local, nbr_offset, conv_weight)))
    sent = pl.pallas_call(
        edge_kernel,
        out_shape=shape(3 * TOK, 128),
        in_specs=[VMEM_SPEC] * 6,
        out_specs=VMEM_SPEC,
        compiler_params=params(24),
        cost_estimate=cost(6e9, 2e6),
        name="edges",
    )(local, mate, other, nbr_offset, conv_weight, inner)

    whole = lambda *dims: pl.BlockSpec(dims, lambda n: (0,) * len(dims))
    d_active, up_high, up_low, cot_turned = pl.pallas_call(
        prepare_kernel,
        grid=(4,),
        out_shape=(
            pltpu.HBM((TOK, FF), F32),
            pltpu.HBM((D, FF), BF16),
            pltpu.HBM((D, FF), BF16),
            pltpu.HBM((2 * D, TOK), BF16),
        ),
        in_specs=[
            whole(TOK, D),
            pl.BlockSpec((D, FF // 4), lambda n: (0, n)),
            pl.BlockSpec((FF // 4, D), lambda n: (n, 0)),
        ],
        out_specs=(
            pl.BlockSpec((TOK, FF // 4), lambda n: (0, n)),
            pl.BlockSpec((D, FF // 4), lambda n: (0, n)),
            pl.BlockSpec((D, FF // 4), lambda n: (0, n)),
            whole(2 * D, TOK),
        ),
        compiler_params=params(20),
        cost_estimate=cost(4e9, 12e6),
        name="prepare",
    )(cotangent[0], w_up, w_down)

    def exchange(values):
        swapped = lax.all_to_all(
            values.reshape(SCENE, 3 * UNITS, 128), SCENE_AXES, split_axis=0, concat_axis=0, tiled=True
        )
        return swapped.reshape(3 * TOK, 128)

    mixed = pl.pallas_call(
        attention_kernel,
        out_shape=shape(3 * TOK, 128),
        in_specs=[VMEM_SPEC] * 4,
        out_specs=VMEM_SPEC,
        scratch_shapes=[pltpu.VMEM((3 * TOK, 128), F32), pltpu.VMEM((TOK, 256), F32)],
        compiler_params=params(24),
        cost_estimate=cost(8e9, 4e6),
        name="attention",
    )(exchange(sent), w_qkv, w_out, score_bias)
    returned = exchange(mixed)

    pair = pltpu.HBM((FF // SUB, 2 * TOK, SUB), BF16)
    hbm = pl.BlockSpec(memory_space=pltpu.HBM)
    middle, active, d_hidden, keep, send = pl.pallas_call(
        gradient_kernel,
        out_shape=(pltpu.HBM((TOK, D), F32), pair, pair, shape(64, 72, 128), shape(64, 72, 128)),
        in_specs=[VMEM_SPEC] * 2 + [hbm] * 4,
        out_specs=(hbm, hbm, hbm, VMEM_SPEC, VMEM_SPEC),
        scratch_shapes=[
            pltpu.VMEM((TOK, FF), F32),
            pltpu.VMEM((D, FF), BF16),
            pltpu.VMEM((D, FF), BF16),
            pltpu.VMEM((2 * D, TOK), BF16),
            pltpu.VMEM((TOK, D), F32),
            pltpu.VMEM((FF // SUB, 2 * TOK, SUB), BF16),
            pltpu.VMEM((FF // SUB, 2 * TOK, SUB), BF16),
            pltpu.VMEM((2 * TOK, D), BF16),
            pltpu.VMEM((2 * D, TOK), BF16),
            pltpu.VMEM((D, FF), F32),
            pltpu.VMEM((D, FF), F32),
            pltpu.SemaphoreType.DMA((4,)),
            pltpu.SemaphoreType.DMA((3,)),
        ],
        compiler_params=params(44),
        cost_estimate=cost(12e9, 16e6),
        name="gradient",
    )(
        sent,
        returned,
        *(
            pltpu.with_memory_space_constraint(a, pltpu.HBM)
            for a in (d_active, up_high, up_low, cot_turned)
        ),
    )
    got = lax.ppermute(send, "c", [(0, 1), (1, 0)])

    block = SUB
    block_out, grad_mid = pl.pallas_call(
        output_kernel,
        grid=(FF // SUB,),
        out_shape=(shape(TOK, D), shape(TOK, D)),
        in_specs=[
            whole(TOK, D),
            whole(TOK, D),
            pl.BlockSpec((1, 2 * TOK, block), lambda n: (n, 0, 0)),
            pl.BlockSpec((1, 2 * TOK, block), lambda n: (n, 0, 0)),
            pl.BlockSpec((D, block), lambda n: (0, n)),
            pl.BlockSpec((block, D), lambda n: (n, 0)),
        ],
        out_specs=(whole(TOK, D), whole(TOK, D)),
        compiler_params=params(24),
        cost_estimate=cost(6e9, 11e6),
        name="outputs",
    )(middle, cotangent[0], active, d_hidden, w_up, w_down)

    pieces = lax.all_to_all(keep + got, CHIP_AXES, split_axis=0, concat_axis=0, tiled=True)
    grad_up, grad_down = pl.pallas_call(
        finish_kernel,
        out_shape=(shape(24, 192), shape(48, 96)),
        in_specs=[VMEM_SPEC],
        out_specs=(VMEM_SPEC, VMEM_SPEC),
        compiler_params=params(8),
        name="finish",
    )(pieces)
    grad_down = grad_down.T
    return block_out[None], grad_mid[None], grad_up, grad_down


def solution(mesh):
    fine = Mesh(mesh.devices.reshape(4, 2, 2, 4, 2), (*SCENE_AXES, *BATCH_AXES))
    slab = P(BATCH_AXES, SCENE_AXES, None)
    shard = P(SCENE_AXES, BATCH_AXES)
    return jax.shard_map(
        on_device,
        mesh=fine,
        in_specs=(slab, P(None, BATCH_AXES, SCENE_AXES), slab, P(), P(), P(), P(), P(), P()),
        out_specs=(slab, slab, shard, shard),
        check_vma=False,
    )
```

```python
import functools

import jax
import jax.numpy as jnp
from jax import lax
from jax.experimental import pallas as pl
from jax.experimental.pallas import tpu as pltpu
from jax.sharding import Mesh
from jax.sharding import PartitionSpec as P

D = 384
FF = 1536
TAPS = 27
HALO = 64
TOK = 384
SCENE = 16
UNITS = 24
SCENE_AXES = ("y", "zh", "c")
BATCH_AXES = ("x", "zl")
CHIP_AXES = ("y", "zh", "x", "zl")
F32 = jnp.float32
BF16 = jnp.bfloat16
NN = (((1,), (0,)), ((), ()))
NT = (((1,), (1,)), ((), ()))
VMEM_SPEC = pl.BlockSpec(memory_space=pltpu.VMEM)
SUB = 256


def params(mebibytes):
    return pltpu.CompilerParams(vmem_limit_bytes=mebibytes * 1024 * 1024)


def cost(flops, moved):
    return pl.CostEstimate(flops=int(flops), bytes_accessed=int(moved), transcendentals=0)


def parts_of(values):
    high = values.astype(BF16)
    return high, (values - high.astype(F32)).astype(BF16)


def dot(a, b, dims=NN):
    return lax.dot_general(a, b, dims, preferred_element_type=F32)


def dot3(a, b, dims=NN):
    return dot(a[0], b[0], dims) + (dot(a[0], b[1], dims) + dot(a[1], b[0], dims))


def stack(values):
    return jnp.concatenate(parts_of(values), axis=0)


def dot_stacked(a, b, dims=NN):
    rows = a.shape[0] // 2
    both = dot(a, b[0], dims)
    return both[:rows] + (both[rows:] + dot(a[:rows], b[1], dims))


def normalise(values):
    average = jnp.mean(values, axis=-1, keepdims=True)
    centered = values - average
    variance = jnp.mean(centered * centered, axis=-1, keepdims=True)
    scale = lax.rsqrt(variance + 1e-05)
    return centered * scale, scale


def slots():
    return [2 * j + k for k in range(2) for j in range(12)]


def from_members(ref):
    rows = []
    for place in slots():
        tiles = [ref[pl.ds(UNITS * t + place, SCENE, stride=3 * UNITS), :] for t in range(3)]
        rows.append(jnp.concatenate(tiles, axis=1))
    return jnp.concatenate(rows, axis=0)


def to_members(ref, values):
    for unit, place in enumerate(slots()):
        for t in range(3):
            ref[pl.ds(UNITS * t + place, SCENE, stride=3 * UNITS), :] = values[
                SCENE * unit : SCENE * (unit + 1), 128 * t : 128 * (t + 1)
            ]


def convolve(tok, ext, offsets, weight_ref):
    middle_tap = TAPS // 2
    taps = [a for a in range(TAPS) if a != middle_tap]
    chunk = 13
    count = tok.shape[0]
    row = lax.broadcasted_iota(jnp.int32, (count, 32), 0)
    lanes = lax.broadcasted_iota(jnp.int32, (count, ext.shape[0]), 1)
    table = jnp.concatenate(parts_of(ext), axis=1)
    index = jnp.where(offsets > HALO, -1, offsets + row + HALO)
    acc = tok + tok * weight_ref[middle_tap : middle_tap + 1, :]
    for start in range(0, len(taps), chunk):
        hits = [
            jnp.where(index[:, a : a + 1] == lanes, 1.0, 0.0).astype(BF16)
            for a in taps[start : start + chunk]
        ]
        picked = dot(jnp.concatenate(hits, axis=0), table)
        for i, a in enumerate(taps[start : start + chunk]):
            piece = picked[count * i : count * (i + 1)]
            acc = acc + (piece[:, :D] + piece[:, D:]) * weight_ref[a : a + 1, :]
    return acc


def offsets_of(nbr_ref):
    return jnp.concatenate([nbr_ref[:, 0, :], jnp.zeros((5, TOK), jnp.int32)], axis=0).T


def inner_kernel(tok_hbm, nbr_hbm, weight_hbm, out_ref, tok_ref, nbr_ref, weight_ref, done):
    copies = [
        pltpu.make_async_copy(tok_hbm, tok_ref, done.at[0]),
        pltpu.make_async_copy(nbr_hbm, nbr_ref, done.at[1]),
        pltpu.make_async_copy(weight_hbm, weight_ref, done.at[2]),
    ]
    for copy in copies:
        copy.start()
    for copy in copies:
        copy.wait()
    offsets = offsets_of(nbr_ref)
    for start in (HALO, HALO + 128):
        out_ref[start - HALO : start - HALO + 128, :] = convolve(
            tok_ref[start : start + 128, :],
            tok_ref[start - HALO : start + 128 + HALO, :],
            offsets[start : start + 128],
            weight_ref,
        )


def edge_kernel(tok_ref, mate_ref, other_ref, nbr_ref, weight_ref, inner_ref, sent_ref):
    even = jnp.full((HALO, D), lax.axis_index("c"), jnp.int32) == 0
    low = jnp.where(even, other_ref[...], mate_ref[...])
    high = jnp.where(even, mate_ref[...], other_ref[...])
    offsets = offsets_of(nbr_ref)
    blank = jnp.zeros((HALO, D), F32)
    head = convolve(
        tok_ref[:HALO, :],
        jnp.concatenate([low, tok_ref[: 2 * HALO, :], blank], axis=0),
        offsets[:HALO],
        weight_ref,
    )
    tail = convolve(
        tok_ref[TOK - HALO :, :],
        jnp.concatenate([tok_ref[TOK - 2 * HALO :, :], high, blank], axis=0),
        offsets[TOK - HALO :],
        weight_ref,
    )
    to_members(sent_ref, jnp.concatenate([head, inner_ref[...], tail], axis=0))


def attention_kernel(got_ref, qkv_ref, wout_ref, bias_ref, sent_ref, rows_ref, scores_ref):
    for place in range(UNITS):
        group, half = place // 2, place % 2
        for t in range(3):
            rows_ref[pl.ds(TOK * t + 32 * group + half, SCENE, stride=2), :] = got_ref[
                pl.ds(UNITS * t + place, SCENE, stride=3 * UNITS), :
            ]
    normed, _ = normalise(
        jnp.concatenate([rows_ref[TOK * t : TOK * (t + 1), :] for t in range(3)], axis=1)
    )
    qkv = dot_stacked(stack(normed), parts_of(qkv_ref[...]))
    head_of = lax.broadcasted_iota(jnp.int32, (16, 128), 1) // 16
    masks = [jnp.where(head_of == h, 1.0, 0.0).astype(BF16) for h in range(8)]
    row_head = (lax.broadcasted_iota(jnp.int32, (256, 128), 0) // 16) % 8
    ones = jnp.where(
        row_head == lax.broadcasted_iota(jnp.int32, (256, 128), 1) // 16, 1.0, 0.0
    ).astype(BF16)
    lane = lax.broadcasted_iota(jnp.int32, (32, 128), 1)
    lowers = [(shift, lane % (2 * shift) < shift) for shift in (8, 4, 2, 1)]

    def spread(values, group):
        pieces = []
        for half in range(2):
            piece = values[32 * group + 16 * half : 32 * group + 16 * half + 16]
            pieces += [piece * mask for mask in masks]
        return jnp.concatenate(pieces, axis=0)

    def score(t):
        cols = slice(128 * t, 128 * (t + 1))
        q_high, q_low = parts_of(qkv[:, :D][:, cols] * 0.25)
        keys = parts_of(qkv[:, D : 2 * D][:, cols])
        bias = jnp.concatenate(
            [bias_ref[8 * t + h][:, 16 * half : 16 * half + 16] for half in range(2) for h in range(8)],
            axis=1,
        )
        for g in range(12):
            rows = slice(32 * g, 32 * g + 32)
            query = jnp.concatenate([q_high[rows], q_low[rows]], axis=0)
            spread_keys = tuple(spread(part, g) for part in keys)
            scores_ref[t, rows, :] = dot_stacked(query, spread_keys, NT) + bias

    def attend(t):
        vals = parts_of(qkv[:, 2 * D :][:, 128 * t : 128 * (t + 1)])
        pieces = []
        for g in range(12):
            rows = slice(32 * g, 32 * g + 32)
            scores = scores_ref[t, rows, :]
            top = jnp.maximum(scores[:, :128], scores[:, 128:])
            for shift, lower in lowers:
                other = jnp.where(lower, pltpu.roll(top, 128 - shift, 1), pltpu.roll(top, shift, 1))
                top = jnp.maximum(top, other)
            weight = jnp.exp(scores - jnp.concatenate([top, top], axis=1))
            w_high, w_low = parts_of(weight)
            v_high, v_low = (spread(part, g) for part in vals)
            wide = jnp.concatenate([v_high, ones], axis=1)
            both = dot(jnp.concatenate([w_high, w_low], axis=0), wide)
            total = both[:32] + both[32:]
            mixed = total[:, :128] + dot(w_high, v_low)
            pieces.append(mixed / total[:, 128:])
        return jnp.concatenate(pieces, axis=0)

    score(0)
    score(1)
    attended = [attend(0)]
    score(2)
    attended += [attend(1), attend(2)]
    attended = jnp.concatenate(attended, axis=1)
    mixed = dot_stacked(stack(attended), parts_of(wout_ref[...]))
    for t in range(3):
        rows_ref[TOK * t : TOK * (t + 1), :] = mixed[:, 128 * t : 128 * (t + 1)]
    for place in range(UNITS):
        group, half = place // 2, place % 2
        for t in range(3):
            sent_ref[pl.ds(UNITS * t + place, SCENE, stride=3 * UNITS), :] = rows_ref[
                pl.ds(TOK * t + 32 * group + half, SCENE, stride=2), :
            ]


def gauss(x):
    z = jnp.clip(x * 0.7071067811865476, -3.832506856900711, 3.832506856900711)
    s = z * z
    top = 0.00022905065861350646
    for c in (0.0034082910107109506, 0.050955695062380861, 0.18520832239976145, 1.128379143519084):
        top = top * s + c
    low = -1.1791602954361697e-7
    for c in (
        0.000023547966471313185,
        0.0010179625278914885,
        0.014070470171167667,
        0.11098505178285362,
        0.49746925110067538,
        1.0,
    ):
        low = low * s + c
    return 0.5 + 0.5 * (z * top / low), 0.3989422804014327 * jnp.exp(-0.5 * (x * x))


def prepare_kernel(cot_ref, up_ref, down_ref, d_active_ref, up_high_ref, up_low_ref, ct_ref):
    @pl.when(pl.program_id(0) == 0)
    def _():
        ct_ref[...] = stack(cot_ref[...].T)

    d_active_ref[...] = dot_stacked(stack(cot_ref[...]), parts_of(down_ref[...]), NT)
    up_high_ref[...], up_low_ref[...] = parts_of(up_ref[...])


def gradient_kernel(
    first_ref, ret_ref, d_active_hbm, up_high_hbm, up_low_hbm, ct_hbm,
    mid_hbm, act_hbm, dh_hbm, keep_ref, send_ref,
    d_active_ref, up_high_ref, up_low_ref, ct_ref, mid_ref, act_ref, dh_ref,
    normed_ref, nt_ref, grad_up_ref, grad_down_ref, came, left,
):
    pairs = (
        (up_high_hbm, up_high_ref),
        (up_low_hbm, up_low_ref),
        (d_active_hbm, d_active_ref),
        (ct_hbm, ct_ref),
    )
    loads = [pltpu.make_async_copy(src, dst, came.at[i]) for i, (src, dst) in enumerate(pairs)]
    for load in loads:
        load.start()
    mid = from_members(first_ref) + from_members(ret_ref)
    mid_ref[...] = mid
    stores = [pltpu.make_async_copy(mid_ref, mid_hbm, left.at[0])]
    stores[0].start()
    normed, _ = normalise(mid)
    normed_ref[...] = stack(normed)
    nt_ref[...] = stack(normed.T)

    def enter(i):
        cols = slice(SUB * i, SUB * (i + 1))
        return dot_stacked(normed_ref[...], (up_high_ref[:, cols], up_low_ref[:, cols]))

    loads[0].wait()
    loads[1].wait()
    count = FF // SUB
    ahead = enter(0)
    loads[2].wait()
    loads[3].wait()
    for i in range(count):
        hidden = ahead
        if i + 1 < count:
            ahead = enter(i + 1)
        here = slice(SUB * i, SUB * (i + 1))
        chance, density = gauss(hidden)
        active = parts_of(hidden * chance)
        d_hidden = parts_of(d_active_ref[:, here] * (chance + hidden * density))
        act_ref[i, :TOK, :], act_ref[i, TOK:, :] = active
        dh_ref[i, :TOK, :], dh_ref[i, TOK:, :] = d_hidden
        grad_down_ref[:, here] = dot_stacked(ct_ref[...], active)
        grad_up_ref[:, here] = dot_stacked(nt_ref[...], d_hidden)
    stores.append(pltpu.make_async_copy(act_ref, act_hbm, left.at[1]))
    stores.append(pltpu.make_async_copy(dh_ref, dh_hbm, left.at[2]))
    stores[1].start()
    stores[2].start()
    pack(grad_up_ref, grad_down_ref, keep_ref, send_ref)
    for store in stores:
        store.wait()


def output_kernel(mid_ref, cot_ref, act_ref, dh_ref, up_ref, down_ref, out_ref, mid_grad_ref):
    step = pl.program_id(0)
    out_part = dot_stacked(act_ref[0], parts_of(down_ref[...]))
    norm_part = dot_stacked(dh_ref[0], parts_of(up_ref[...]), NT)

    @pl.when(step == 0)
    def _():
        out_ref[...] = mid_ref[...] + out_part
        mid_grad_ref[...] = norm_part

    @pl.when(step > 0)
    def _():
        out_ref[...] += out_part
        mid_grad_ref[...] += norm_part

    @pl.when(step == pl.num_programs(0) - 1)
    def _():
        normed, scale = normalise(mid_ref[...])
        d_normed = mid_grad_ref[...]
        shift = jnp.mean(d_normed, axis=-1, keepdims=True)
        slope = jnp.mean(d_normed * normed, axis=-1, keepdims=True)
        mid_grad_ref[...] = cot_ref[...] + scale * (d_normed - shift - normed * slope)


def pack(grad_up_ref, grad_down_ref, keep_ref, send_ref):
    core = lax.axis_index("c")
    lane = lax.broadcasted_iota(jnp.int32, (8, 128), 1)
    left = lane < 64
    segment = lane // 32

    def piece(quarter, sigma, g, beta, turned):
        row = pl.multiple_of((4 * quarter + sigma) * 24, 8)

        def up_tile(i, t):
            return grad_up_ref[pl.ds(row + 8 * i, 8), 384 * g + 128 * t : 384 * g + 128 * (t + 1)]

        def down_tile(i, t):
            col = pl.multiple_of(384 * quarter + 128 * t, 128)
            start = 96 * g + 48 * beta + 8 * i
            return grad_down_ref[start : start + 8, pl.ds(col, 128)]

        full = [up_tile(i, 2 * beta) for i in range(3)]
        m0, m2 = up_tile(0, 1), up_tile(2, 1)
        own = left if beta == 0 else jnp.logical_not(left)
        if sigma == 0:
            c = [down_tile(i, 0) for i in range(6)]
        elif sigma == 1:
            c = [jnp.where(segment == 3, down_tile(i, 0), down_tile(i, 1)) for i in range(6)]
        elif sigma == 2:
            c = [jnp.where(segment == 0, down_tile(i, 2), down_tile(i, 1)) for i in range(6)]
        else:
            c = [down_tile(i, 2) for i in range(6)]
        free = 3 - sigma
        hole = segment == free
        start = 2 if beta == 0 else 0
        turn = 32 * ((start - (free + 2)) % 4)
        extra = pltpu.roll(c[4], turn, 1) if turn else c[4]
        return full + [
            jnp.where(own, m0, turned),
            jnp.where(own, m2, extra),
            jnp.where(hole, pltpu.roll(c[5], 96, 1), c[0]),
            jnp.where(hole, pltpu.roll(c[5], 64, 1), c[1]),
            jnp.where(hole, pltpu.roll(c[5], 32, 1), c[2]),
            jnp.where(hole, pltpu.roll(c[4], 96, 1), c[3]),
        ]

    def lay(even_ref, odd_ref):
        def body(quarter, carry):
            for g in range(4):
                for sigma in range(4):
                    row = pl.multiple_of((4 * quarter + sigma) * 24 + 8, 8)
                    turned = pltpu.roll(
                        grad_up_ref[pl.ds(row, 8), 384 * g + 128 : 384 * g + 256], 64, 1
                    )
                    for beta in range(2):
                        ref = odd_ref if sigma % 2 else even_ref
                        where = (2 * quarter + sigma // 2) * 8 + 2 * g + beta
                        for i, rows in enumerate(piece(quarter, sigma, g, beta, turned)):
                            ref[where, 8 * i : 8 * (i + 1), :] = rows
            return carry

        lax.fori_loop(0, 4, body, 0)

    @pl.when(core == 0)
    def _():
        lay(keep_ref, send_ref)

    @pl.when(core == 1)
    def _():
        lay(send_ref, keep_ref)


def finish_kernel(pieces_ref, up_ref, down_ref):
    scale = (TOK * 128) ** -0.5
    sums = []
    for k in range(4):
        total = pieces_ref[16 * k]
        for i in range(1, 16):
            total = total + pieces_ref[16 * k + i]
        sums.append(total)
    z = (sums[0] + sums[1]) + (sums[2] + sums[3])
    z = z * scale
    beta = lax.axis_index("zl")
    sigma = 2 * lax.axis_index("zh") + lax.axis_index("c")
    lane = lax.broadcasted_iota(jnp.int32, (8, 128), 1)
    lane24 = lax.broadcasted_iota(jnp.int32, (24, 128), 1)
    even24 = jnp.full((24, 128), beta, jnp.int32) == 0
    even = jnp.full((8, 128), beta, jnp.int32) == 0
    full, a, b = z[:24], z[24:32], z[32:40]
    turned = pltpu.roll(a, 64, 1)
    half = jnp.concatenate(
        [
            jnp.where(even, a, turned),
            jnp.where(even, turned, a),
            jnp.where(even, b, pltpu.roll(b, 64, 1)),
        ],
        axis=0,
    )
    swapped = pltpu.roll(full, 64, 1)
    up_ref[:, :128] = jnp.where(even24, full, jnp.where(lane24 < 64, half, swapped))
    up_ref[:, 128:] = jnp.where(even24, half, swapped)[:, :64]
    rest = z[40:]
    turned_rest = rest
    for k in range(1, 4):
        chosen = jnp.full((32, 128), sigma, jnp.int32) == k
        turned_rest = jnp.where(chosen, pltpu.roll(rest, 32 * k, 1), turned_rest)
    p0, p1, p2, p3 = [turned_rest[8 * i : 8 * (i + 1)] for i in range(4)]
    segment = lane // 32
    c5 = jnp.where(
        segment == 0,
        pltpu.roll(p0, 32, 1),
        jnp.where(segment == 1, pltpu.roll(p1, 64, 1), pltpu.roll(p2, 96, 1)),
    )
    tail = jnp.where(even, pltpu.roll(b, 96, 1), pltpu.roll(b, 32, 1))
    c4 = jnp.where(segment == 0, pltpu.roll(p3, 32, 1), tail)
    down_ref[...] = jnp.concatenate([p0, p1, p2, p3, c4, c5], axis=0)[:, :96]


def shape(*dims):
    return jax.ShapeDtypeStruct(dims, F32)


def on_device(tokens, nbr_offset, cotangent, conv_weight, w_qkv, w_out, score_bias, w_up, w_down):
    local = tokens[0]
    mates = [(i, i ^ 1) for i in range(SCENE)]
    others = [(i, i + 1) for i in range(1, SCENE - 1, 2)]
    others += [(target, source) for source, target in others]
    even = lax.axis_index("c") == 0
    head, tail = local[:HALO], local[TOK - HALO :]
    other = lax.ppermute(jnp.where(even, head, tail), SCENE_AXES, others)
    mate = lax.ppermute(jnp.where(even, tail, head), SCENE_AXES, mates)

    inner = pl.pallas_call(
        inner_kernel,
        out_shape=shape(256, D),
        in_specs=[pl.BlockSpec(memory_space=pltpu.HBM)] * 3,
        out_specs=VMEM_SPEC,
        scratch_shapes=[
            pltpu.VMEM((TOK, D), F32),
            pltpu.VMEM((TAPS, 1, TOK), jnp.int32),
            pltpu.VMEM((TAPS, D), F32),
            pltpu.SemaphoreType.DMA((3,)),
        ],
        compiler_params=params(16),
        cost_estimate=cost(3e9, 1e6),
        name="inner",
    )(*(pltpu.with_memory_space_constraint(a, pltpu.HBM) for a in (local, nbr_offset, conv_weight)))
    sent = pl.pallas_call(
        edge_kernel,
        out_shape=shape(3 * TOK, 128),
        in_specs=[VMEM_SPEC] * 6,
        out_specs=VMEM_SPEC,
        compiler_params=params(24),
        cost_estimate=cost(6e9, 2e6),
        name="edges",
    )(local, mate, other, nbr_offset, conv_weight, inner)

    whole = lambda *dims: pl.BlockSpec(dims, lambda n: (0,) * len(dims))
    d_active, up_high, up_low, cot_turned = pl.pallas_call(
        prepare_kernel,
        grid=(4,),
        out_shape=(
            pltpu.HBM((TOK, FF), F32),
            pltpu.HBM((D, FF), BF16),
            pltpu.HBM((D, FF), BF16),
            pltpu.HBM((2 * D, TOK), BF16),
        ),
        in_specs=[
            whole(TOK, D),
            pl.BlockSpec((D, FF // 4), lambda n: (0, n)),
            pl.BlockSpec((FF // 4, D), lambda n: (n, 0)),
        ],
        out_specs=(
            pl.BlockSpec((TOK, FF // 4), lambda n: (0, n)),
            pl.BlockSpec((D, FF // 4), lambda n: (0, n)),
            pl.BlockSpec((D, FF // 4), lambda n: (0, n)),
            whole(2 * D, TOK),
        ),
        compiler_params=params(20),
        cost_estimate=cost(4e9, 12e6),
        name="prepare",
    )(cotangent[0], w_up, w_down)

    def exchange(values):
        swapped = lax.all_to_all(
            values.reshape(SCENE, 3 * UNITS, 128), SCENE_AXES, split_axis=0, concat_axis=0, tiled=True
        )
        return swapped.reshape(3 * TOK, 128)

    mixed = pl.pallas_call(
        attention_kernel,
        out_shape=shape(3 * TOK, 128),
        in_specs=[VMEM_SPEC] * 4,
        out_specs=VMEM_SPEC,
        scratch_shapes=[pltpu.VMEM((3 * TOK, 128), F32), pltpu.VMEM((3, TOK, 256), F32)],
        compiler_params=params(24),
        cost_estimate=cost(8e9, 4e6),
        name="attention",
    )(exchange(sent), w_qkv, w_out, score_bias)
    returned = exchange(mixed)

    pair = pltpu.HBM((FF // SUB, 2 * TOK, SUB), BF16)
    hbm = pl.BlockSpec(memory_space=pltpu.HBM)
    middle, active, d_hidden, keep, send = pl.pallas_call(
        gradient_kernel,
        out_shape=(pltpu.HBM((TOK, D), F32), pair, pair, shape(64, 72, 128), shape(64, 72, 128)),
        in_specs=[VMEM_SPEC] * 2 + [hbm] * 4,
        out_specs=(hbm, hbm, hbm, VMEM_SPEC, VMEM_SPEC),
        scratch_shapes=[
            pltpu.VMEM((TOK, FF), F32),
            pltpu.VMEM((D, FF), BF16),
            pltpu.VMEM((D, FF), BF16),
            pltpu.VMEM((2 * D, TOK), BF16),
            pltpu.VMEM((TOK, D), F32),
            pltpu.VMEM((FF // SUB, 2 * TOK, SUB), BF16),
            pltpu.VMEM((FF // SUB, 2 * TOK, SUB), BF16),
            pltpu.VMEM((2 * TOK, D), BF16),
            pltpu.VMEM((2 * D, TOK), BF16),
            pltpu.VMEM((D, FF), F32),
            pltpu.VMEM((D, FF), F32),
            pltpu.SemaphoreType.DMA((4,)),
            pltpu.SemaphoreType.DMA((3,)),
        ],
        compiler_params=params(44),
        cost_estimate=cost(12e9, 16e6),
        name="gradient",
    )(
        sent,
        returned,
        *(
            pltpu.with_memory_space_constraint(a, pltpu.HBM)
            for a in (d_active, up_high, up_low, cot_turned)
        ),
    )
    got = lax.ppermute(send, "c", [(0, 1), (1, 0)])

    block = SUB
    block_out, grad_mid = pl.pallas_call(
        output_kernel,
        grid=(FF // SUB,),
        out_shape=(shape(TOK, D), shape(TOK, D)),
        in_specs=[
            whole(TOK, D),
            whole(TOK, D),
            pl.BlockSpec((1, 2 * TOK, block), lambda n: (n, 0, 0)),
            pl.BlockSpec((1, 2 * TOK, block), lambda n: (n, 0, 0)),
            pl.BlockSpec((D, block), lambda n: (0, n)),
            pl.BlockSpec((block, D), lambda n: (n, 0)),
        ],
        out_specs=(whole(TOK, D), whole(TOK, D)),
        compiler_params=params(24),
        cost_estimate=cost(6e9, 11e6),
        name="outputs",
    )(middle, cotangent[0], active, d_hidden, w_up, w_down)

    pieces = lax.all_to_all(keep + got, CHIP_AXES, split_axis=0, concat_axis=0, tiled=True)
    grad_up, grad_down = pl.pallas_call(
        finish_kernel,
        out_shape=(shape(24, 192), shape(48, 96)),
        in_specs=[VMEM_SPEC],
        out_specs=(VMEM_SPEC, VMEM_SPEC),
        compiler_params=params(8),
        name="finish",
    )(pieces)
    grad_down = grad_down.T
    return block_out[None], grad_mid[None], grad_up, grad_down


def solution(mesh):
    fine = Mesh(mesh.devices.reshape(4, 2, 2, 4, 2), (*SCENE_AXES, *BATCH_AXES))
    slab = P(BATCH_AXES, SCENE_AXES, None)
    shard = P(SCENE_AXES, BATCH_AXES)
    return jax.shard_map(
        on_device,
        mesh=fine,
        in_specs=(slab, P(None, BATCH_AXES, SCENE_AXES), slab, P(), P(), P(), P(), P(), P()),
        out_specs=(slab, slab, shard, shard),
        check_vma=False,
    )
```

```python
import functools

import jax
import jax.numpy as jnp
from jax import lax
from jax.experimental import pallas as pl
from jax.experimental.pallas import tpu as pltpu
from jax.sharding import Mesh
from jax.sharding import PartitionSpec as P

D = 384
FF = 1536
TAPS = 27
HALO = 64
TOK = 384
SCENE = 16
UNITS = 24
SCENE_AXES = ("y", "zh", "c")
BATCH_AXES = ("x", "zl")
CHIP_AXES = ("y", "zh", "x", "zl")
F32 = jnp.float32
BF16 = jnp.bfloat16
NN = (((1,), (0,)), ((), ()))
NT = (((1,), (1,)), ((), ()))
VMEM_SPEC = pl.BlockSpec(memory_space=pltpu.VMEM)
SUB = 512


def params(mebibytes):
    return pltpu.CompilerParams(vmem_limit_bytes=mebibytes * 1024 * 1024)


def cost(flops, moved):
    return pl.CostEstimate(flops=int(flops), bytes_accessed=int(moved), transcendentals=0)


def parts_of(values):
    high = values.astype(BF16)
    return high, (values - high.astype(F32)).astype(BF16)


def dot(a, b, dims=NN):
    return lax.dot_general(a, b, dims, preferred_element_type=F32)


def dot3(a, b, dims=NN):
    return dot(a[0], b[0], dims) + (dot(a[0], b[1], dims) + dot(a[1], b[0], dims))


def stack(values):
    return jnp.concatenate(parts_of(values), axis=0)


def dot_stacked(a, b, dims=NN):
    rows = a.shape[0] // 2
    both = dot(a, b[0], dims)
    return both[:rows] + (both[rows:] + dot(a[:rows], b[1], dims))


def normalise(values):
    average = jnp.mean(values, axis=-1, keepdims=True)
    centered = values - average
    variance = jnp.mean(centered * centered, axis=-1, keepdims=True)
    scale = lax.rsqrt(variance + 1e-05)
    return centered * scale, scale


def slots():
    return [2 * j + k for k in range(2) for j in range(12)]


def from_members(ref):
    rows = []
    for place in slots():
        tiles = [ref[pl.ds(UNITS * t + place, SCENE, stride=3 * UNITS), :] for t in range(3)]
        rows.append(jnp.concatenate(tiles, axis=1))
    return jnp.concatenate(rows, axis=0)


def to_members(ref, values):
    for unit, place in enumerate(slots()):
        for t in range(3):
            ref[pl.ds(UNITS * t + place, SCENE, stride=3 * UNITS), :] = values[
                SCENE * unit : SCENE * (unit + 1), 128 * t : 128 * (t + 1)
            ]


def convolve(tok, ext, offsets, weight_ref):
    middle_tap = TAPS // 2
    taps = [a for a in range(TAPS) if a != middle_tap]
    chunk = 13
    count = tok.shape[0]
    row = lax.broadcasted_iota(jnp.int32, (count, 32), 0)
    lanes = lax.broadcasted_iota(jnp.int32, (count, ext.shape[0]), 1)
    table = jnp.concatenate(parts_of(ext), axis=1)
    index = jnp.where(offsets > HALO, -1, offsets + row + HALO)
    acc = tok + tok * weight_ref[middle_tap : middle_tap + 1, :]
    for start in range(0, len(taps), chunk):
        hits = [
            jnp.where(index[:, a : a + 1] == lanes, 1.0, 0.0).astype(BF16)
            for a in taps[start : start + chunk]
        ]
        picked = dot(jnp.concatenate(hits, axis=0), table)
        for i, a in enumerate(taps[start : start + chunk]):
            piece = picked[count * i : count * (i + 1)]
            acc = acc + (piece[:, :D] + piece[:, D:]) * weight_ref[a : a + 1, :]
    return acc


def offsets_of(nbr_ref):
    return jnp.concatenate([nbr_ref[:, 0, :], jnp.zeros((5, TOK), jnp.int32)], axis=0).T


def inner_kernel(tok_hbm, nbr_hbm, weight_hbm, out_ref, tok_ref, nbr_ref, weight_ref, done):
    copies = [
        pltpu.make_async_copy(tok_hbm, tok_ref, done.at[0]),
        pltpu.make_async_copy(nbr_hbm, nbr_ref, done.at[1]),
        pltpu.make_async_copy(weight_hbm, weight_ref, done.at[2]),
    ]
    for copy in copies:
        copy.start()
    for copy in copies:
        copy.wait()
    offsets = offsets_of(nbr_ref)
    for start in (HALO, HALO + 128):
        out_ref[start - HALO : start - HALO + 128, :] = convolve(
            tok_ref[start : start + 128, :],
            tok_ref[start - HALO : start + 128 + HALO, :],
            offsets[start : start + 128],
            weight_ref,
        )


def edge_kernel(tok_ref, mate_ref, other_ref, nbr_ref, weight_ref, inner_ref, sent_ref):
    even = jnp.full((HALO, D), lax.axis_index("c"), jnp.int32) == 0
    low = jnp.where(even, other_ref[...], mate_ref[...])
    high = jnp.where(even, mate_ref[...], other_ref[...])
    offsets = offsets_of(nbr_ref)
    blank = jnp.zeros((HALO, D), F32)
    head = convolve(
        tok_ref[:HALO, :],
        jnp.concatenate([low, tok_ref[: 2 * HALO, :], blank], axis=0),
        offsets[:HALO],
        weight_ref,
    )
    tail = convolve(
        tok_ref[TOK - HALO :, :],
        jnp.concatenate([tok_ref[TOK - 2 * HALO :, :], high, blank], axis=0),
        offsets[TOK - HALO :],
        weight_ref,
    )
    to_members(sent_ref, jnp.concatenate([head, inner_ref[...], tail], axis=0))


def attention_kernel(got_ref, qkv_ref, wout_ref, bias_ref, sent_ref, rows_ref, scores_ref):
    for place in range(UNITS):
        group, half = place // 2, place % 2
        for t in range(3):
            rows_ref[pl.ds(TOK * t + 32 * group + half, SCENE, stride=2), :] = got_ref[
                pl.ds(UNITS * t + place, SCENE, stride=3 * UNITS), :
            ]
    normed, _ = normalise(
        jnp.concatenate([rows_ref[TOK * t : TOK * (t + 1), :] for t in range(3)], axis=1)
    )
    qkv = dot_stacked(stack(normed), parts_of(qkv_ref[...]))
    head_of = lax.broadcasted_iota(jnp.int32, (16, 128), 1) // 16
    masks = [jnp.where(head_of == h, 1.0, 0.0).astype(BF16) for h in range(8)]
    row_head = (lax.broadcasted_iota(jnp.int32, (256, 128), 0) // 16) % 8
    ones = jnp.where(
        row_head == lax.broadcasted_iota(jnp.int32, (256, 128), 1) // 16, 1.0, 0.0
    ).astype(BF16)
    lane = lax.broadcasted_iota(jnp.int32, (32, 128), 1)
    lowers = [(shift, lane % (2 * shift) < shift) for shift in (8, 4, 2, 1)]

    def spread(values, group):
        pieces = []
        for half in range(2):
            piece = values[32 * group + 16 * half : 32 * group + 16 * half + 16]
            pieces += [piece * mask for mask in masks]
        return jnp.concatenate(pieces, axis=0)

    def score(t):
        cols = slice(128 * t, 128 * (t + 1))
        q_high, q_low = parts_of(qkv[:, :D][:, cols] * 0.25)
        keys = parts_of(qkv[:, D : 2 * D][:, cols])
        bias = jnp.concatenate(
            [bias_ref[8 * t + h][:, 16 * half : 16 * half + 16] for half in range(2) for h in range(8)],
            axis=1,
        )
        for g in range(12):
            rows = slice(32 * g, 32 * g + 32)
            query = jnp.concatenate([q_high[rows], q_low[rows]], axis=0)
            spread_keys = tuple(spread(part, g) for part in keys)
            scores_ref[t, rows, :] = dot_stacked(query, spread_keys, NT) + bias

    def attend(t):
        vals = parts_of(qkv[:, 2 * D :][:, 128 * t : 128 * (t + 1)])
        pieces = []
        for g in range(12):
            rows = slice(32 * g, 32 * g + 32)
            scores = scores_ref[t, rows, :]
            top = jnp.maximum(scores[:, :128], scores[:, 128:])
            for shift, lower in lowers:
                other = jnp.where(lower, pltpu.roll(top, 128 - shift, 1), pltpu.roll(top, shift, 1))
                top = jnp.maximum(top, other)
            weight = jnp.exp(scores - jnp.concatenate([top, top], axis=1))
            w_high, w_low = parts_of(weight)
            v_high, v_low = (spread(part, g) for part in vals)
            wide = jnp.concatenate([v_high, ones], axis=1)
            both = dot(jnp.concatenate([w_high, w_low], axis=0), wide)
            total = both[:32] + both[32:]
            mixed = total[:, :128] + dot(w_high, v_low)
            pieces.append(mixed / total[:, 128:])
        return jnp.concatenate(pieces, axis=0)

    score(0)
    score(1)
    attended = [attend(0)]
    score(2)
    attended += [attend(1), attend(2)]
    attended = jnp.concatenate(attended, axis=1)
    mixed = dot_stacked(stack(attended), parts_of(wout_ref[...]))
    for t in range(3):
        rows_ref[TOK * t : TOK * (t + 1), :] = mixed[:, 128 * t : 128 * (t + 1)]
    for place in range(UNITS):
        group, half = place // 2, place % 2
        for t in range(3):
            sent_ref[pl.ds(UNITS * t + place, SCENE, stride=3 * UNITS), :] = rows_ref[
                pl.ds(TOK * t + 32 * group + half, SCENE, stride=2), :
            ]


def gauss(x):
    z = jnp.clip(x * 0.7071067811865476, -3.832506856900711, 3.832506856900711)
    s = z * z
    top = 0.00022905065861350646
    for c in (0.0034082910107109506, 0.050955695062380861, 0.18520832239976145, 1.128379143519084):
        top = top * s + c
    low = -1.1791602954361697e-7
    for c in (
        0.000023547966471313185,
        0.0010179625278914885,
        0.014070470171167667,
        0.11098505178285362,
        0.49746925110067538,
        1.0,
    ):
        low = low * s + c
    return 0.5 + 0.5 * (z * top / low), 0.3989422804014327 * jnp.exp(-0.5 * (x * x))


def prepare_kernel(cot_ref, up_ref, down_ref, d_active_ref, up_high_ref, up_low_ref, ct_ref):
    @pl.when(pl.program_id(0) == 0)
    def _():
        ct_ref[...] = stack(cot_ref[...].T)

    d_active_ref[...] = dot_stacked(stack(cot_ref[...]), parts_of(down_ref[...]), NT)
    up_high_ref[...], up_low_ref[...] = parts_of(up_ref[...])


def gradient_kernel(
    first_ref, ret_ref, d_active_hbm, up_high_hbm, up_low_hbm, ct_hbm,
    mid_hbm, act_hbm, dh_hbm, keep_ref, send_ref,
    d_active_ref, up_high_ref, up_low_ref, ct_ref, mid_ref, act_ref, dh_ref,
    normed_ref, nt_ref, grad_up_ref, grad_down_ref, came, left,
):
    pairs = (
        (up_high_hbm, up_high_ref),
        (up_low_hbm, up_low_ref),
        (d_active_hbm, d_active_ref),
        (ct_hbm, ct_ref),
    )
    loads = [pltpu.make_async_copy(src, dst, came.at[i]) for i, (src, dst) in enumerate(pairs)]
    for load in loads:
        load.start()
    mid = from_members(first_ref) + from_members(ret_ref)
    mid_ref[...] = mid
    stores = [pltpu.make_async_copy(mid_ref, mid_hbm, left.at[0])]
    stores[0].start()
    normed, _ = normalise(mid)
    normed_ref[...] = stack(normed)
    nt_ref[...] = stack(normed.T)

    def enter(i):
        cols = slice(SUB * i, SUB * (i + 1))
        return dot_stacked(normed_ref[...], (up_high_ref[:, cols], up_low_ref[:, cols]))

    loads[0].wait()
    loads[1].wait()
    count = FF // SUB
    ahead = enter(0)
    loads[2].wait()
    loads[3].wait()
    for i in range(count):
        hidden = ahead
        if i + 1 < count:
            ahead = enter(i + 1)
        here = slice(SUB * i, SUB * (i + 1))
        chance, density = gauss(hidden)
        active = parts_of(hidden * chance)
        d_hidden = parts_of(d_active_ref[:, here] * (chance + hidden * density))
        act_ref[i, :TOK, :], act_ref[i, TOK:, :] = active
        dh_ref[i, :TOK, :], dh_ref[i, TOK:, :] = d_hidden
        grad_down_ref[:, here] = dot_stacked(ct_ref[...], active)
        grad_up_ref[:, here] = dot_stacked(nt_ref[...], d_hidden)
    stores.append(pltpu.make_async_copy(act_ref, act_hbm, left.at[1]))
    stores.append(pltpu.make_async_copy(dh_ref, dh_hbm, left.at[2]))
    stores[1].start()
    stores[2].start()
    pack(grad_up_ref, grad_down_ref, keep_ref, send_ref)
    for store in stores:
        store.wait()


def output_kernel(mid_ref, cot_ref, act_ref, dh_ref, up_ref, down_ref, out_ref, mid_grad_ref):
    step = pl.program_id(0)
    out_part = dot_stacked(act_ref[0], parts_of(down_ref[...]))
    norm_part = dot_stacked(dh_ref[0], parts_of(up_ref[...]), NT)

    @pl.when(step == 0)
    def _():
        out_ref[...] = mid_ref[...] + out_part
        mid_grad_ref[...] = norm_part

    @pl.when(step > 0)
    def _():
        out_ref[...] += out_part
        mid_grad_ref[...] += norm_part

    @pl.when(step == pl.num_programs(0) - 1)
    def _():
        normed, scale = normalise(mid_ref[...])
        d_normed = mid_grad_ref[...]
        shift = jnp.mean(d_normed, axis=-1, keepdims=True)
        slope = jnp.mean(d_normed * normed, axis=-1, keepdims=True)
        mid_grad_ref[...] = cot_ref[...] + scale * (d_normed - shift - normed * slope)


def pack(grad_up_ref, grad_down_ref, keep_ref, send_ref):
    core = lax.axis_index("c")
    lane = lax.broadcasted_iota(jnp.int32, (8, 128), 1)
    left = lane < 64
    segment = lane // 32

    def piece(quarter, sigma, g, beta, turned):
        row = pl.multiple_of((4 * quarter + sigma) * 24, 8)

        def up_tile(i, t):
            return grad_up_ref[pl.ds(row + 8 * i, 8), 384 * g + 128 * t : 384 * g + 128 * (t + 1)]

        def down_tile(i, t):
            col = pl.multiple_of(384 * quarter + 128 * t, 128)
            start = 96 * g + 48 * beta + 8 * i
            return grad_down_ref[start : start + 8, pl.ds(col, 128)]

        full = [up_tile(i, 2 * beta) for i in range(3)]
        m0, m2 = up_tile(0, 1), up_tile(2, 1)
        own = left if beta == 0 else jnp.logical_not(left)
        if sigma == 0:
            c = [down_tile(i, 0) for i in range(6)]
        elif sigma == 1:
            c = [jnp.where(segment == 3, down_tile(i, 0), down_tile(i, 1)) for i in range(6)]
        elif sigma == 2:
            c = [jnp.where(segment == 0, down_tile(i, 2), down_tile(i, 1)) for i in range(6)]
        else:
            c = [down_tile(i, 2) for i in range(6)]
        free = 3 - sigma
        hole = segment == free
        start = 2 if beta == 0 else 0
        turn = 32 * ((start - (free + 2)) % 4)
        extra = pltpu.roll(c[4], turn, 1) if turn else c[4]
        return full + [
            jnp.where(own, m0, turned),
            jnp.where(own, m2, extra),
            jnp.where(hole, pltpu.roll(c[5], 96, 1), c[0]),
            jnp.where(hole, pltpu.roll(c[5], 64, 1), c[1]),
            jnp.where(hole, pltpu.roll(c[5], 32, 1), c[2]),
            jnp.where(hole, pltpu.roll(c[4], 96, 1), c[3]),
        ]

    def lay(even_ref, odd_ref):
        def body(quarter, carry):
            for g in range(4):
                for sigma in range(4):
                    row = pl.multiple_of((4 * quarter + sigma) * 24 + 8, 8)
                    turned = pltpu.roll(
                        grad_up_ref[pl.ds(row, 8), 384 * g + 128 : 384 * g + 256], 64, 1
                    )
                    for beta in range(2):
                        ref = odd_ref if sigma % 2 else even_ref
                        where = (2 * quarter + sigma // 2) * 8 + 2 * g + beta
                        for i, rows in enumerate(piece(quarter, sigma, g, beta, turned)):
                            ref[where, 8 * i : 8 * (i + 1), :] = rows
            return carry

        lax.fori_loop(0, 4, body, 0)

    @pl.when(core == 0)
    def _():
        lay(keep_ref, send_ref)

    @pl.when(core == 1)
    def _():
        lay(send_ref, keep_ref)


def finish_kernel(pieces_ref, up_ref, down_ref):
    scale = (TOK * 128) ** -0.5
    sums = []
    for k in range(4):
        total = pieces_ref[16 * k]
        for i in range(1, 16):
            total = total + pieces_ref[16 * k + i]
        sums.append(total)
    z = (sums[0] + sums[1]) + (sums[2] + sums[3])
    z = z * scale
    beta = lax.axis_index("zl")
    sigma = 2 * lax.axis_index("zh") + lax.axis_index("c")
    lane = lax.broadcasted_iota(jnp.int32, (8, 128), 1)
    lane24 = lax.broadcasted_iota(jnp.int32, (24, 128), 1)
    even24 = jnp.full((24, 128), beta, jnp.int32) == 0
    even = jnp.full((8, 128), beta, jnp.int32) == 0
    full, a, b = z[:24], z[24:32], z[32:40]
    turned = pltpu.roll(a, 64, 1)
    half = jnp.concatenate(
        [
            jnp.where(even, a, turned),
            jnp.where(even, turned, a),
            jnp.where(even, b, pltpu.roll(b, 64, 1)),
        ],
        axis=0,
    )
    swapped = pltpu.roll(full, 64, 1)
    up_ref[:, :128] = jnp.where(even24, full, jnp.where(lane24 < 64, half, swapped))
    up_ref[:, 128:] = jnp.where(even24, half, swapped)[:, :64]
    rest = z[40:]
    turned_rest = rest
    for k in range(1, 4):
        chosen = jnp.full((32, 128), sigma, jnp.int32) == k
        turned_rest = jnp.where(chosen, pltpu.roll(rest, 32 * k, 1), turned_rest)
    p0, p1, p2, p3 = [turned_rest[8 * i : 8 * (i + 1)] for i in range(4)]
    segment = lane // 32
    c5 = jnp.where(
        segment == 0,
        pltpu.roll(p0, 32, 1),
        jnp.where(segment == 1, pltpu.roll(p1, 64, 1), pltpu.roll(p2, 96, 1)),
    )
    tail = jnp.where(even, pltpu.roll(b, 96, 1), pltpu.roll(b, 32, 1))
    c4 = jnp.where(segment == 0, pltpu.roll(p3, 32, 1), tail)
    down_ref[...] = jnp.concatenate([p0, p1, p2, p3, c4, c5], axis=0)[:, :96]


def shape(*dims):
    return jax.ShapeDtypeStruct(dims, F32)


def on_device(tokens, nbr_offset, cotangent, conv_weight, w_qkv, w_out, score_bias, w_up, w_down):
    local = tokens[0]
    mates = [(i, i ^ 1) for i in range(SCENE)]
    others = [(i, i + 1) for i in range(1, SCENE - 1, 2)]
    others += [(target, source) for source, target in others]
    even = lax.axis_index("c") == 0
    head, tail = local[:HALO], local[TOK - HALO :]
    other = lax.ppermute(jnp.where(even, head, tail), SCENE_AXES, others)
    mate = lax.ppermute(jnp.where(even, tail, head), SCENE_AXES, mates)

    inner = pl.pallas_call(
        inner_kernel,
        out_shape=shape(256, D),
        in_specs=[pl.BlockSpec(memory_space=pltpu.HBM)] * 3,
        out_specs=VMEM_SPEC,
        scratch_shapes=[
            pltpu.VMEM((TOK, D), F32),
            pltpu.VMEM((TAPS, 1, TOK), jnp.int32),
            pltpu.VMEM((TAPS, D), F32),
            pltpu.SemaphoreType.DMA((3,)),
        ],
        compiler_params=params(16),
        cost_estimate=cost(3e9, 1e6),
        name="inner",
    )(*(pltpu.with_memory_space_constraint(a, pltpu.HBM) for a in (local, nbr_offset, conv_weight)))
    sent = pl.pallas_call(
        edge_kernel,
        out_shape=shape(3 * TOK, 128),
        in_specs=[VMEM_SPEC] * 6,
        out_specs=VMEM_SPEC,
        compiler_params=params(24),
        cost_estimate=cost(6e9, 2e6),
        name="edges",
    )(local, mate, other, nbr_offset, conv_weight, inner)

    whole = lambda *dims: pl.BlockSpec(dims, lambda n: (0,) * len(dims))
    d_active, up_high, up_low, cot_turned = pl.pallas_call(
        prepare_kernel,
        grid=(4,),
        out_shape=(
            pltpu.HBM((TOK, FF), F32),
            pltpu.HBM((D, FF), BF16),
            pltpu.HBM((D, FF), BF16),
            pltpu.HBM((2 * D, TOK), BF16),
        ),
        in_specs=[
            whole(TOK, D),
            pl.BlockSpec((D, FF // 4), lambda n: (0, n)),
            pl.BlockSpec((FF // 4, D), lambda n: (n, 0)),
        ],
        out_specs=(
            pl.BlockSpec((TOK, FF // 4), lambda n: (0, n)),
            pl.BlockSpec((D, FF // 4), lambda n: (0, n)),
            pl.BlockSpec((D, FF // 4), lambda n: (0, n)),
            whole(2 * D, TOK),
        ),
        compiler_params=params(20),
        cost_estimate=cost(4e9, 12e6),
        name="prepare",
    )(cotangent[0], w_up, w_down)

    def exchange(values):
        swapped = lax.all_to_all(
            values.reshape(SCENE, 3 * UNITS, 128), SCENE_AXES, split_axis=0, concat_axis=0, tiled=True
        )
        return swapped.reshape(3 * TOK, 128)

    mixed = pl.pallas_call(
        attention_kernel,
        out_shape=shape(3 * TOK, 128),
        in_specs=[VMEM_SPEC] * 4,
        out_specs=VMEM_SPEC,
        scratch_shapes=[pltpu.VMEM((3 * TOK, 128), F32), pltpu.VMEM((3, TOK, 256), F32)],
        compiler_params=params(24),
        cost_estimate=cost(8e9, 4e6),
        name="attention",
    )(exchange(sent), w_qkv, w_out, score_bias)
    returned = exchange(mixed)

    pair = pltpu.HBM((FF // SUB, 2 * TOK, SUB), BF16)
    hbm = pl.BlockSpec(memory_space=pltpu.HBM)
    middle, active, d_hidden, keep, send = pl.pallas_call(
        gradient_kernel,
        out_shape=(pltpu.HBM((TOK, D), F32), pair, pair, shape(64, 72, 128), shape(64, 72, 128)),
        in_specs=[VMEM_SPEC] * 2 + [hbm] * 4,
        out_specs=(hbm, hbm, hbm, VMEM_SPEC, VMEM_SPEC),
        scratch_shapes=[
            pltpu.VMEM((TOK, FF), F32),
            pltpu.VMEM((D, FF), BF16),
            pltpu.VMEM((D, FF), BF16),
            pltpu.VMEM((2 * D, TOK), BF16),
            pltpu.VMEM((TOK, D), F32),
            pltpu.VMEM((FF // SUB, 2 * TOK, SUB), BF16),
            pltpu.VMEM((FF // SUB, 2 * TOK, SUB), BF16),
            pltpu.VMEM((2 * TOK, D), BF16),
            pltpu.VMEM((2 * D, TOK), BF16),
            pltpu.VMEM((D, FF), F32),
            pltpu.VMEM((D, FF), F32),
            pltpu.SemaphoreType.DMA((4,)),
            pltpu.SemaphoreType.DMA((3,)),
        ],
        compiler_params=params(44),
        cost_estimate=cost(12e9, 16e6),
        name="gradient",
    )(
        sent,
        returned,
        *(
            pltpu.with_memory_space_constraint(a, pltpu.HBM)
            for a in (d_active, up_high, up_low, cot_turned)
        ),
    )
    got = lax.ppermute(send, "c", [(0, 1), (1, 0)])

    block = SUB
    block_out, grad_mid = pl.pallas_call(
        output_kernel,
        grid=(FF // SUB,),
        out_shape=(shape(TOK, D), shape(TOK, D)),
        in_specs=[
            whole(TOK, D),
            whole(TOK, D),
            pl.BlockSpec((1, 2 * TOK, block), lambda n: (n, 0, 0)),
            pl.BlockSpec((1, 2 * TOK, block), lambda n: (n, 0, 0)),
            pl.BlockSpec((D, block), lambda n: (0, n)),
            pl.BlockSpec((block, D), lambda n: (n, 0)),
        ],
        out_specs=(whole(TOK, D), whole(TOK, D)),
        compiler_params=params(24),
        cost_estimate=cost(6e9, 11e6),
        name="outputs",
    )(middle, cotangent[0], active, d_hidden, w_up, w_down)

    pieces = lax.all_to_all(keep + got, CHIP_AXES, split_axis=0, concat_axis=0, tiled=True)
    grad_up, grad_down = pl.pallas_call(
        finish_kernel,
        out_shape=(shape(24, 192), shape(48, 96)),
        in_specs=[VMEM_SPEC],
        out_specs=(VMEM_SPEC, VMEM_SPEC),
        compiler_params=params(8),
        name="finish",
    )(pieces)
    grad_down = grad_down.T
    return block_out[None], grad_mid[None], grad_up, grad_down


def solution(mesh):
    fine = Mesh(mesh.devices.reshape(4, 2, 2, 4, 2), (*SCENE_AXES, *BATCH_AXES))
    slab = P(BATCH_AXES, SCENE_AXES, None)
    shard = P(SCENE_AXES, BATCH_AXES)
    return jax.shard_map(
        on_device,
        mesh=fine,
        in_specs=(slab, P(None, BATCH_AXES, SCENE_AXES), slab, P(), P(), P(), P(), P(), P()),
        out_specs=(slab, slab, shard, shard),
        check_vma=False,
    )
```

```python
import functools

import jax
import jax.numpy as jnp
from jax import lax
from jax.experimental import pallas as pl
from jax.experimental.pallas import tpu as pltpu
from jax.sharding import Mesh
from jax.sharding import PartitionSpec as P

D = 384
FF = 1536
TAPS = 27
HALO = 64
TOK = 384
SCENE = 16
UNITS = 24
SCENE_AXES = ("y", "zh", "c")
BATCH_AXES = ("x", "zl")
CHIP_AXES = ("y", "zh", "x", "zl")
F32 = jnp.float32
BF16 = jnp.bfloat16
NN = (((1,), (0,)), ((), ()))
NT = (((1,), (1,)), ((), ()))
VMEM_SPEC = pl.BlockSpec(memory_space=pltpu.VMEM)
SUB = 512


def params(mebibytes):
    return pltpu.CompilerParams(vmem_limit_bytes=mebibytes * 1024 * 1024)


def cost(flops, moved):
    return pl.CostEstimate(flops=int(flops), bytes_accessed=int(moved), transcendentals=0)


def parts_of(values):
    high = values.astype(BF16)
    return high, (values - high.astype(F32)).astype(BF16)


def dot(a, b, dims=NN):
    return lax.dot_general(a, b, dims, preferred_element_type=F32)


def dot3(a, b, dims=NN):
    return dot(a[0], b[0], dims) + (dot(a[0], b[1], dims) + dot(a[1], b[0], dims))


def stack(values):
    return jnp.concatenate(parts_of(values), axis=0)


def dot_stacked(a, b, dims=NN):
    rows = a.shape[0] // 2
    both = dot(a, b[0], dims)
    return both[:rows] + (both[rows:] + dot(a[:rows], b[1], dims))


def normalise(values):
    average = jnp.mean(values, axis=-1, keepdims=True)
    centered = values - average
    variance = jnp.mean(centered * centered, axis=-1, keepdims=True)
    scale = lax.rsqrt(variance + 1e-05)
    return centered * scale, scale


def slots():
    return [2 * j + k for k in range(2) for j in range(12)]


def from_members(ref):
    rows = []
    for place in slots():
        tiles = [ref[pl.ds(UNITS * t + place, SCENE, stride=3 * UNITS), :] for t in range(3)]
        rows.append(jnp.concatenate(tiles, axis=1))
    return jnp.concatenate(rows, axis=0)


def to_members(ref, values):
    for unit, place in enumerate(slots()):
        for t in range(3):
            ref[pl.ds(UNITS * t + place, SCENE, stride=3 * UNITS), :] = values[
                SCENE * unit : SCENE * (unit + 1), 128 * t : 128 * (t + 1)
            ]


def convolve(tok, ext, offsets, weight_ref):
    middle_tap = TAPS // 2
    taps = [a for a in range(TAPS) if a != middle_tap]
    chunk = 13
    count = tok.shape[0]
    row = lax.broadcasted_iota(jnp.int32, (count, 32), 0)
    lanes = lax.broadcasted_iota(jnp.int32, (count, ext.shape[0]), 1)
    table = jnp.concatenate(parts_of(ext), axis=1)
    index = jnp.where(offsets > HALO, -1, offsets + row + HALO)
    acc = tok + tok * weight_ref[middle_tap : middle_tap + 1, :]
    for start in range(0, len(taps), chunk):
        hits = [
            jnp.where(index[:, a : a + 1] == lanes, 1.0, 0.0).astype(BF16)
            for a in taps[start : start + chunk]
        ]
        picked = dot(jnp.concatenate(hits, axis=0), table)
        for i, a in enumerate(taps[start : start + chunk]):
            piece = picked[count * i : count * (i + 1)]
            acc = acc + (piece[:, :D] + piece[:, D:]) * weight_ref[a : a + 1, :]
    return acc


def offsets_of(nbr_ref):
    return jnp.concatenate([nbr_ref[:, 0, :], jnp.zeros((5, TOK), jnp.int32)], axis=0).T


def inner_kernel(tok_hbm, nbr_hbm, weight_hbm, out_ref, tok_ref, nbr_ref, weight_ref, done):
    copies = [
        pltpu.make_async_copy(tok_hbm, tok_ref, done.at[0]),
        pltpu.make_async_copy(nbr_hbm, nbr_ref, done.at[1]),
        pltpu.make_async_copy(weight_hbm, weight_ref, done.at[2]),
    ]
    for copy in copies:
        copy.start()
    for copy in copies:
        copy.wait()
    offsets = offsets_of(nbr_ref)
    for start in (HALO, HALO + 128):
        out_ref[start - HALO : start - HALO + 128, :] = convolve(
            tok_ref[start : start + 128, :],
            tok_ref[start - HALO : start + 128 + HALO, :],
            offsets[start : start + 128],
            weight_ref,
        )


def edge_kernel(tok_ref, mate_ref, other_ref, nbr_ref, weight_ref, inner_ref, sent_ref):
    even = jnp.full((HALO, D), lax.axis_index("c"), jnp.int32) == 0
    low = jnp.where(even, other_ref[...], mate_ref[...])
    high = jnp.where(even, mate_ref[...], other_ref[...])
    offsets = offsets_of(nbr_ref)
    blank = jnp.zeros((HALO, D), F32)
    head = convolve(
        tok_ref[:HALO, :],
        jnp.concatenate([low, tok_ref[: 2 * HALO, :], blank], axis=0),
        offsets[:HALO],
        weight_ref,
    )
    tail = convolve(
        tok_ref[TOK - HALO :, :],
        jnp.concatenate([tok_ref[TOK - 2 * HALO :, :], high, blank], axis=0),
        offsets[TOK - HALO :],
        weight_ref,
    )
    to_members(sent_ref, jnp.concatenate([head, inner_ref[...], tail], axis=0))


def attention_kernel(got_ref, qkv_ref, wout_ref, bias_ref, sent_ref, rows_ref, scores_ref):
    for place in range(UNITS):
        group, half = place // 2, place % 2
        for t in range(3):
            rows_ref[pl.ds(TOK * t + 32 * group + half, SCENE, stride=2), :] = got_ref[
                pl.ds(UNITS * t + place, SCENE, stride=3 * UNITS), :
            ]
    normed, _ = normalise(
        jnp.concatenate([rows_ref[TOK * t : TOK * (t + 1), :] for t in range(3)], axis=1)
    )
    qkv = dot_stacked(stack(normed), parts_of(qkv_ref[...]))
    head_of = lax.broadcasted_iota(jnp.int32, (16, 128), 1) // 16
    masks = [jnp.where(head_of == h, 1.0, 0.0).astype(BF16) for h in range(8)]
    row_head = (lax.broadcasted_iota(jnp.int32, (256, 128), 0) // 16) % 8
    ones = jnp.where(
        row_head == lax.broadcasted_iota(jnp.int32, (256, 128), 1) // 16, 1.0, 0.0
    ).astype(BF16)
    lane = lax.broadcasted_iota(jnp.int32, (32, 128), 1)
    lowers = [(shift, lane % (2 * shift) < shift) for shift in (8, 4, 2, 1)]

    def spread(values, group):
        pieces = []
        for half in range(2):
            piece = values[32 * group + 16 * half : 32 * group + 16 * half + 16]
            pieces += [piece * mask for mask in masks]
        return jnp.concatenate(pieces, axis=0)

    def score(t):
        cols = slice(128 * t, 128 * (t + 1))
        q_high, q_low = parts_of(qkv[:, :D][:, cols] * 0.25)
        keys = parts_of(qkv[:, D : 2 * D][:, cols])
        bias = jnp.concatenate(
            [bias_ref[8 * t + h][:, 16 * half : 16 * half + 16] for half in range(2) for h in range(8)],
            axis=1,
        )
        for g in range(12):
            rows = slice(32 * g, 32 * g + 32)
            query = jnp.concatenate([q_high[rows], q_low[rows]], axis=0)
            spread_keys = tuple(spread(part, g) for part in keys)
            scores_ref[t, rows, :] = dot_stacked(query, spread_keys, NT) + bias

    def attend(t):
        vals = parts_of(qkv[:, 2 * D :][:, 128 * t : 128 * (t + 1)])
        pieces = []
        for g in range(12):
            rows = slice(32 * g, 32 * g + 32)
            scores = scores_ref[t, rows, :]
            top = jnp.maximum(scores[:, :128], scores[:, 128:])
            for shift, lower in lowers:
                other = jnp.where(lower, pltpu.roll(top, 128 - shift, 1), pltpu.roll(top, shift, 1))
                top = jnp.maximum(top, other)
            weight = jnp.exp(scores - jnp.concatenate([top, top], axis=1))
            w_high, w_low = parts_of(weight)
            v_high, v_low = (spread(part, g) for part in vals)
            wide = jnp.concatenate([v_high, ones], axis=1)
            both = dot(jnp.concatenate([w_high, w_low], axis=0), wide)
            total = both[:32] + both[32:]
            mixed = total[:, :128] + dot(w_high, v_low)
            pieces.append(mixed / total[:, 128:])
        return jnp.concatenate(pieces, axis=0)

    score(0)
    score(1)
    attended = [attend(0)]
    score(2)
    attended += [attend(1), attend(2)]
    attended = jnp.concatenate(attended, axis=1)
    mixed = dot_stacked(stack(attended), parts_of(wout_ref[...]))
    for t in range(3):
        rows_ref[TOK * t : TOK * (t + 1), :] = mixed[:, 128 * t : 128 * (t + 1)]
    for place in range(UNITS):
        group, half = place // 2, place % 2
        for t in range(3):
            sent_ref[pl.ds(UNITS * t + place, SCENE, stride=3 * UNITS), :] = rows_ref[
                pl.ds(TOK * t + 32 * group + half, SCENE, stride=2), :
            ]


def gauss(x):
    z = jnp.clip(x * 0.7071067811865476, -3.832506856900711, 3.832506856900711)
    s = z * z
    top = 0.00022905065861350646
    for c in (0.0034082910107109506, 0.050955695062380861, 0.18520832239976145, 1.128379143519084):
        top = top * s + c
    low = -1.1791602954361697e-7
    for c in (
        0.000023547966471313185,
        0.0010179625278914885,
        0.014070470171167667,
        0.11098505178285362,
        0.49746925110067538,
        1.0,
    ):
        low = low * s + c
    return 0.5 + 0.5 * (z * top / low), 0.3989422804014327 * jnp.exp(-0.5 * (x * x))


def prepare_kernel(cot_ref, up_ref, down_ref, d_active_ref, up_high_ref, up_low_ref, ct_ref):
    @pl.when(pl.program_id(0) == 0)
    def _():
        ct_ref[...] = stack(cot_ref[...].T)

    d_active_ref[...] = dot_stacked(stack(cot_ref[...]), parts_of(down_ref[...]), NT)
    up_high_ref[...], up_low_ref[...] = parts_of(up_ref[...])


def gradient_kernel(
    first_ref, ret_ref, d_active_hbm, up_high_hbm, up_low_hbm, ct_hbm,
    mid_hbm, act_hbm, dh_hbm, keep_ref, send_ref,
    d_active_ref, up_high_ref, up_low_ref, ct_ref, mid_ref, act_ref, dh_ref,
    normed_ref, nt_ref, grad_up_ref, grad_down_ref, came, left,
):
    pairs = (
        (up_high_hbm, up_high_ref),
        (up_low_hbm, up_low_ref),
        (d_active_hbm, d_active_ref),
        (ct_hbm, ct_ref),
    )
    loads = [pltpu.make_async_copy(src, dst, came.at[i]) for i, (src, dst) in enumerate(pairs)]
    for load in loads:
        load.start()
    mid = from_members(first_ref) + from_members(ret_ref)
    mid_ref[...] = mid
    stores = [pltpu.make_async_copy(mid_ref, mid_hbm, left.at[0])]
    stores[0].start()
    normed, _ = normalise(mid)
    normed_ref[...] = stack(normed)
    nt_ref[...] = stack(normed.T)

    def enter(i):
        cols = slice(SUB * i, SUB * (i + 1))
        return dot_stacked(normed_ref[...], (up_high_ref[:, cols], up_low_ref[:, cols]))

    loads[0].wait()
    loads[1].wait()
    count = FF // SUB
    ahead = enter(0)
    loads[2].wait()
    loads[3].wait()
    for i in range(count):
        hidden = ahead
        if i + 1 < count:
            ahead = enter(i + 1)
        here = slice(SUB * i, SUB * (i + 1))
        chance, density = gauss(hidden)
        active = parts_of(hidden * chance)
        d_hidden = parts_of(d_active_ref[:, here] * (chance + hidden * density))
        act_ref[i, :TOK, :], act_ref[i, TOK:, :] = active
        dh_ref[i, :TOK, :], dh_ref[i, TOK:, :] = d_hidden
        grad_down_ref[:, here] = dot_stacked(ct_ref[...], active)
        grad_up_ref[:, here] = dot_stacked(nt_ref[...], d_hidden)
        for ref, hbm, k in ((act_ref, act_hbm, 1 + 2 * i), (dh_ref, dh_hbm, 2 + 2 * i)):
            stores.append(pltpu.make_async_copy(ref.at[i], hbm.at[i], left.at[k]))
            stores[-1].start()
    pack(grad_up_ref, grad_down_ref, keep_ref, send_ref)
    for store in stores:
        store.wait()


def output_kernel(mid_ref, cot_ref, act_ref, dh_ref, up_ref, down_ref, out_ref, mid_grad_ref):
    step = pl.program_id(0)
    out_part = dot_stacked(act_ref[0], parts_of(down_ref[...]))
    norm_part = dot_stacked(dh_ref[0], parts_of(up_ref[...]), NT)

    @pl.when(step == 0)
    def _():
        out_ref[...] = mid_ref[...] + out_part
        mid_grad_ref[...] = norm_part

    @pl.when(step > 0)
    def _():
        out_ref[...] += out_part
        mid_grad_ref[...] += norm_part

    @pl.when(step == pl.num_programs(0) - 1)
    def _():
        normed, scale = normalise(mid_ref[...])
        d_normed = mid_grad_ref[...]
        shift = jnp.mean(d_normed, axis=-1, keepdims=True)
        slope = jnp.mean(d_normed * normed, axis=-1, keepdims=True)
        mid_grad_ref[...] = cot_ref[...] + scale * (d_normed - shift - normed * slope)


def pack(grad_up_ref, grad_down_ref, keep_ref, send_ref):
    core = lax.axis_index("c")
    lane = lax.broadcasted_iota(jnp.int32, (8, 128), 1)
    left = lane < 64
    segment = lane // 32

    def piece(quarter, sigma, g, beta, turned):
        row = pl.multiple_of((4 * quarter + sigma) * 24, 8)

        def up_tile(i, t):
            return grad_up_ref[pl.ds(row + 8 * i, 8), 384 * g + 128 * t : 384 * g + 128 * (t + 1)]

        def down_tile(i, t):
            col = pl.multiple_of(384 * quarter + 128 * t, 128)
            start = 96 * g + 48 * beta + 8 * i
            return grad_down_ref[start : start + 8, pl.ds(col, 128)]

        full = [up_tile(i, 2 * beta) for i in range(3)]
        m0, m2 = up_tile(0, 1), up_tile(2, 1)
        own = left if beta == 0 else jnp.logical_not(left)
        if sigma == 0:
            c = [down_tile(i, 0) for i in range(6)]
        elif sigma == 1:
            c = [jnp.where(segment == 3, down_tile(i, 0), down_tile(i, 1)) for i in range(6)]
        elif sigma == 2:
            c = [jnp.where(segment == 0, down_tile(i, 2), down_tile(i, 1)) for i in range(6)]
        else:
            c = [down_tile(i, 2) for i in range(6)]
        free = 3 - sigma
        hole = segment == free
        start = 2 if beta == 0 else 0
        turn = 32 * ((start - (free + 2)) % 4)
        extra = pltpu.roll(c[4], turn, 1) if turn else c[4]
        return full + [
            jnp.where(own, m0, turned),
            jnp.where(own, m2, extra),
            jnp.where(hole, pltpu.roll(c[5], 96, 1), c[0]),
            jnp.where(hole, pltpu.roll(c[5], 64, 1), c[1]),
            jnp.where(hole, pltpu.roll(c[5], 32, 1), c[2]),
            jnp.where(hole, pltpu.roll(c[4], 96, 1), c[3]),
        ]

    def lay(even_ref, odd_ref):
        def body(quarter, carry):
            for g in range(4):
                for sigma in range(4):
                    row = pl.multiple_of((4 * quarter + sigma) * 24 + 8, 8)
                    turned = pltpu.roll(
                        grad_up_ref[pl.ds(row, 8), 384 * g + 128 : 384 * g + 256], 64, 1
                    )
                    for beta in range(2):
                        ref = odd_ref if sigma % 2 else even_ref
                        where = (2 * quarter + sigma // 2) * 8 + 2 * g + beta
                        for i, rows in enumerate(piece(quarter, sigma, g, beta, turned)):
                            ref[where, 8 * i : 8 * (i + 1), :] = rows
            return carry

        lax.fori_loop(0, 4, body, 0)

    @pl.when(core == 0)
    def _():
        lay(keep_ref, send_ref)

    @pl.when(core == 1)
    def _():
        lay(send_ref, keep_ref)


def finish_kernel(pieces_ref, up_ref, down_ref):
    scale = (TOK * 128) ** -0.5
    sums = []
    for k in range(4):
        total = pieces_ref[16 * k]
        for i in range(1, 16):
            total = total + pieces_ref[16 * k + i]
        sums.append(total)
    z = (sums[0] + sums[1]) + (sums[2] + sums[3])
    z = z * scale
    beta = lax.axis_index("zl")
    sigma = 2 * lax.axis_index("zh") + lax.axis_index("c")
    lane = lax.broadcasted_iota(jnp.int32, (8, 128), 1)
    lane24 = lax.broadcasted_iota(jnp.int32, (24, 128), 1)
    even24 = jnp.full((24, 128), beta, jnp.int32) == 0
    even = jnp.full((8, 128), beta, jnp.int32) == 0
    full, a, b = z[:24], z[24:32], z[32:40]
    turned = pltpu.roll(a, 64, 1)
    half = jnp.concatenate(
        [
            jnp.where(even, a, turned),
            jnp.where(even, turned, a),
            jnp.where(even, b, pltpu.roll(b, 64, 1)),
        ],
        axis=0,
    )
    swapped = pltpu.roll(full, 64, 1)
    up_ref[:, :128] = jnp.where(even24, full, jnp.where(lane24 < 64, half, swapped))
    up_ref[:, 128:] = jnp.where(even24, half, swapped)[:, :64]
    rest = z[40:]
    turned_rest = rest
    for k in range(1, 4):
        chosen = jnp.full((32, 128), sigma, jnp.int32) == k
        turned_rest = jnp.where(chosen, pltpu.roll(rest, 32 * k, 1), turned_rest)
    p0, p1, p2, p3 = [turned_rest[8 * i : 8 * (i + 1)] for i in range(4)]
    segment = lane // 32
    c5 = jnp.where(
        segment == 0,
        pltpu.roll(p0, 32, 1),
        jnp.where(segment == 1, pltpu.roll(p1, 64, 1), pltpu.roll(p2, 96, 1)),
    )
    tail = jnp.where(even, pltpu.roll(b, 96, 1), pltpu.roll(b, 32, 1))
    c4 = jnp.where(segment == 0, pltpu.roll(p3, 32, 1), tail)
    down_ref[...] = jnp.concatenate([p0, p1, p2, p3, c4, c5], axis=0)[:, :96]


def shape(*dims):
    return jax.ShapeDtypeStruct(dims, F32)


def on_device(tokens, nbr_offset, cotangent, conv_weight, w_qkv, w_out, score_bias, w_up, w_down):
    local = tokens[0]
    mates = [(i, i ^ 1) for i in range(SCENE)]
    others = [(i, i + 1) for i in range(1, SCENE - 1, 2)]
    others += [(target, source) for source, target in others]
    even = lax.axis_index("c") == 0
    head, tail = local[:HALO], local[TOK - HALO :]
    other = lax.ppermute(jnp.where(even, head, tail), SCENE_AXES, others)
    mate = lax.ppermute(jnp.where(even, tail, head), SCENE_AXES, mates)

    inner = pl.pallas_call(
        inner_kernel,
        out_shape=shape(256, D),
        in_specs=[pl.BlockSpec(memory_space=pltpu.HBM)] * 3,
        out_specs=VMEM_SPEC,
        scratch_shapes=[
            pltpu.VMEM((TOK, D), F32),
            pltpu.VMEM((TAPS, 1, TOK), jnp.int32),
            pltpu.VMEM((TAPS, D), F32),
            pltpu.SemaphoreType.DMA((3,)),
        ],
        compiler_params=params(16),
        cost_estimate=cost(3e9, 1e6),
        name="inner",
    )(*(pltpu.with_memory_space_constraint(a, pltpu.HBM) for a in (local, nbr_offset, conv_weight)))
    sent = pl.pallas_call(
        edge_kernel,
        out_shape=shape(3 * TOK, 128),
        in_specs=[VMEM_SPEC] * 6,
        out_specs=VMEM_SPEC,
        compiler_params=params(24),
        cost_estimate=cost(6e9, 2e6),
        name="edges",
    )(local, mate, other, nbr_offset, conv_weight, inner)

    whole = lambda *dims: pl.BlockSpec(dims, lambda n: (0,) * len(dims))
    d_active, up_high, up_low, cot_turned = pl.pallas_call(
        prepare_kernel,
        grid=(4,),
        out_shape=(
            pltpu.HBM((TOK, FF), F32),
            pltpu.HBM((D, FF), BF16),
            pltpu.HBM((D, FF), BF16),
            pltpu.HBM((2 * D, TOK), BF16),
        ),
        in_specs=[
            whole(TOK, D),
            pl.BlockSpec((D, FF // 4), lambda n: (0, n)),
            pl.BlockSpec((FF // 4, D), lambda n: (n, 0)),
        ],
        out_specs=(
            pl.BlockSpec((TOK, FF // 4), lambda n: (0, n)),
            pl.BlockSpec((D, FF // 4), lambda n: (0, n)),
            pl.BlockSpec((D, FF // 4), lambda n: (0, n)),
            whole(2 * D, TOK),
        ),
        compiler_params=params(20),
        cost_estimate=cost(4e9, 12e6),
        name="prepare",
    )(cotangent[0], w_up, w_down)

    def exchange(values):
        swapped = lax.all_to_all(
            values.reshape(SCENE, 3 * UNITS, 128), SCENE_AXES, split_axis=0, concat_axis=0, tiled=True
        )
        return swapped.reshape(3 * TOK, 128)

    mixed = pl.pallas_call(
        attention_kernel,
        out_shape=shape(3 * TOK, 128),
        in_specs=[VMEM_SPEC] * 4,
        out_specs=VMEM_SPEC,
        scratch_shapes=[pltpu.VMEM((3 * TOK, 128), F32), pltpu.VMEM((3, TOK, 256), F32)],
        compiler_params=params(24),
        cost_estimate=cost(8e9, 4e6),
        name="attention",
    )(exchange(sent), w_qkv, w_out, score_bias)
    returned = exchange(mixed)

    pair = pltpu.HBM((FF // SUB, 2 * TOK, SUB), BF16)
    hbm = pl.BlockSpec(memory_space=pltpu.HBM)
    middle, active, d_hidden, keep, send = pl.pallas_call(
        gradient_kernel,
        out_shape=(pltpu.HBM((TOK, D), F32), pair, pair, shape(64, 72, 128), shape(64, 72, 128)),
        in_specs=[VMEM_SPEC] * 2 + [hbm] * 4,
        out_specs=(hbm, hbm, hbm, VMEM_SPEC, VMEM_SPEC),
        scratch_shapes=[
            pltpu.VMEM((TOK, FF), F32),
            pltpu.VMEM((D, FF), BF16),
            pltpu.VMEM((D, FF), BF16),
            pltpu.VMEM((2 * D, TOK), BF16),
            pltpu.VMEM((TOK, D), F32),
            pltpu.VMEM((FF // SUB, 2 * TOK, SUB), BF16),
            pltpu.VMEM((FF // SUB, 2 * TOK, SUB), BF16),
            pltpu.VMEM((2 * TOK, D), BF16),
            pltpu.VMEM((2 * D, TOK), BF16),
            pltpu.VMEM((D, FF), F32),
            pltpu.VMEM((D, FF), F32),
            pltpu.SemaphoreType.DMA((4,)),
            pltpu.SemaphoreType.DMA((1 + 2 * (FF // SUB),)),
        ],
        compiler_params=params(44),
        cost_estimate=cost(12e9, 16e6),
        name="gradient",
    )(
        sent,
        returned,
        *(
            pltpu.with_memory_space_constraint(a, pltpu.HBM)
            for a in (d_active, up_high, up_low, cot_turned)
        ),
    )
    got = lax.ppermute(send, "c", [(0, 1), (1, 0)])

    block = SUB
    block_out, grad_mid = pl.pallas_call(
        output_kernel,
        grid=(FF // SUB,),
        out_shape=(shape(TOK, D), shape(TOK, D)),
        in_specs=[
            whole(TOK, D),
            whole(TOK, D),
            pl.BlockSpec((1, 2 * TOK, block), lambda n: (n, 0, 0)),
            pl.BlockSpec((1, 2 * TOK, block), lambda n: (n, 0, 0)),
            pl.BlockSpec((D, block), lambda n: (0, n)),
            pl.BlockSpec((block, D), lambda n: (n, 0)),
        ],
        out_specs=(whole(TOK, D), whole(TOK, D)),
        compiler_params=params(24),
        cost_estimate=cost(6e9, 11e6),
        name="outputs",
    )(middle, cotangent[0], active, d_hidden, w_up, w_down)

    pieces = lax.all_to_all(keep + got, CHIP_AXES, split_axis=0, concat_axis=0, tiled=True)
    grad_up, grad_down = pl.pallas_call(
        finish_kernel,
        out_shape=(shape(24, 192), shape(48, 96)),
        in_specs=[VMEM_SPEC],
        out_specs=(VMEM_SPEC, VMEM_SPEC),
        compiler_params=params(8),
        name="finish",
    )(pieces)
    grad_down = grad_down.T
    return block_out[None], grad_mid[None], grad_up, grad_down


def solution(mesh):
    fine = Mesh(mesh.devices.reshape(4, 2, 2, 4, 2), (*SCENE_AXES, *BATCH_AXES))
    slab = P(BATCH_AXES, SCENE_AXES, None)
    shard = P(SCENE_AXES, BATCH_AXES)
    return jax.shard_map(
        on_device,
        mesh=fine,
        in_specs=(slab, P(None, BATCH_AXES, SCENE_AXES), slab, P(), P(), P(), P(), P(), P()),
        out_specs=(slab, slab, shard, shard),
        check_vma=False,
    )
```
